128 devices in a mesh: tm: 8 (over y_lo, z), rows: 16 (over x, y_hi, core).
Axes of the slice: x: 4, y: 4 (y_hi: 2, y_lo: 2; y = y_hi * 2 + y_lo), z: 4, core: 2. Of those that a mesh axis runs over, the one named last changes fastest.
Arguments:
- features: bfloat16 [8, 64, 104, 384], P('tm', 'rows'), may hold values from -45 to 45
- conv_cache: bfloat16 [2, 64, 104, 384], P(None, 'rows'), may hold values from -6 to 6
- head_cache: bfloat16 [2, 64, 104, 384], P(None, 'rows'), may hold values from -6 to 6
- conv_weight: bfloat16 [3, 3, 3, 384, 384], replicated, may hold values from -0.0625 to 0.0625
- head_weight: bfloat16 [3, 3, 3, 384, 16], replicated, may hold values from -0.0625 to 0.0625
- patch_weight: bfloat16 [2, 2, 16, 5120], replicated, may hold values from -0.75 to 0.75
- qkv_weight: bfloat16 [5120, 3, 5120], P(None, None, 'rows'), may hold values from -0.078125 to 0.078125
Outputs:
- qkv: bfloat16 [13312, 3, 5120], P('tm', None, 'rows')
The draws below stay inside these ranges and needn't reach their ends.
All inputs are finite; a program needn't handle non-finite values.
Results may differ from the reference program's by a relative error of at most 0.02.
Values may be sent and summed in bfloat16 or wider, within the bound.
No kernel may reach another device: no remote copies, remote signals or barrier semaphores. Data moves between devices by JAX's collectives and lax.ppermute only.
A program may use at most 128 MiB of HBM per device.

```python
import math
import jax
import jax.numpy as jnp
from jax import lax

C = 384
Z = 16
D = 5120
COLS = 104
FRAMES = 8
HEIGHT = 64


def draw_features(key, part):
    key_base, key_pixel, key_channel = jax.random.split(key, 3)
    shape = (FRAMES, HEIGHT, COLS, C)
    base = jnp.clip(jax.random.normal(key_base, shape, jnp.float32), -5.0, 5.0)
    pixel = jnp.exp(jax.random.uniform(key_pixel, (FRAMES, HEIGHT, COLS, 1), jnp.float32, math.log(0.3), math.log(3.0)))
    channel = jnp.exp(jax.random.uniform(key_channel, (C,), jnp.float32, math.log(0.3), math.log(3.0)))
    return (base * pixel * channel).astype(jnp.bfloat16)


def shard_levels(own_key, shape, pieces, low, largest):
    level, own = 1.0, jax.random.fold_in(own_key, 6)
    for axis_at, shards_of in pieces:
        draws = jnp.exp(jax.random.uniform(jax.random.fold_in(own, axis_at), (shards_of,), jnp.float32, low / len(pieces), largest / len(pieces)))
        level = level * jnp.repeat(draws, shape[axis_at] // shards_of).reshape([-1 if axis == axis_at else 1 for axis in range(len(shape))])
    return level


def noise(rng, extent, width, most, cuts=(), dtype=jnp.bfloat16):
    level = shard_levels(rng, extent, cuts, -0.22, 0.18) if cuts else 1.0
    values = jax.random.normal(rng, extent, jnp.float32) * width * level
    return jnp.minimum(jnp.maximum(values, -most), most).astype(dtype)


def setup_inputs(seed: int = 0) -> dict:
    key_of = jax.random.split(jax.random.key(seed), 8)
    features = draw_features(jax.random.fold_in(key_of[7], 71), 0)
    conv_cache = noise(key_of[1], (2, HEIGHT, COLS, C), 1.0, 6.0, ((1, 16),))
    head_cache = noise(key_of[2], (2, HEIGHT, COLS, C), 1.0, 6.0, ((1, 16),))
    conv_weight = noise(key_of[3], (3, 3, 3, C, C), (27 * C) ** -0.5, 0.0625)
    head_weight = noise(key_of[4], (3, 3, 3, C, Z), (27 * C) ** -0.5, 0.0625)
    patch_weight = noise(key_of[5], (2, 2, Z, D), (4 * Z) ** -0.5, 0.75)
    qkv_weight = noise(key_of[6], (D, 3, D), D ** -0.5, 0.078125, ((2, 16),))
    return {"features": features, "conv_cache": conv_cache, "head_cache": head_cache, "conv_weight": conv_weight, "head_weight": head_weight, "patch_weight": patch_weight, "qkv_weight": qkv_weight}


def rms_silu(tensor_in):
    values = tensor_in.astype(jnp.float32)
    scaled = values * lax.rsqrt(lax.optimization_barrier(jnp.mean(values * values, axis=-1, keepdims=True)) + 1e-06)
    return jax.nn.silu(scaled).astype(jnp.bfloat16)

def causal_conv(field, cache_frames, kernel):
    whole = jnp.concatenate([cache_frames, field], axis=0)
    output = lax.conv_general_dilated(whole[None].astype(jnp.float32), kernel.astype(jnp.float32), (1, 1, 1), ((0, 0), (1, 1), (1, 1)), dimension_numbers=('NDHWC', 'DHWIO', 'NDHWC'), precision=lax.Precision.HIGHEST)
    return output[0]

def embed_norm(patch_rows, flat_patch):
    embedded = jnp.dot(patch_rows, flat_patch, preferred_element_type=jnp.float32)
    centred = embedded - lax.optimization_barrier(jnp.mean(embedded, axis=-1, keepdims=True))
    variance = lax.optimization_barrier(jnp.mean(centred * centred, axis=-1, keepdims=True))
    return (centred * lax.rsqrt(variance + 1e-06)).astype(jnp.bfloat16)

def reference(features, conv_cache, head_cache, conv_weight, head_weight, patch_weight, qkv_weight):
    normed_in = rms_silu(features)
    update = causal_conv(normed_in, conv_cache, conv_weight)
    residual = (features.astype(jnp.float32) + update).astype(jnp.bfloat16)
    normed_out = rms_silu(residual)
    latents = causal_conv(normed_out, head_cache, head_weight).astype(jnp.bfloat16)
    frame_count, height, col_count, latent_dim = latents.shape
    patches = latents.reshape(frame_count, height // 2, 2, col_count // 2, 2, latent_dim)
    patches = patches.transpose(0, 1, 3, 2, 4, 5).reshape(frame_count, -1, 4 * latent_dim)
    flat_patch = patch_weight.reshape(4 * latent_dim, -1)
    model_width = qkv_weight.shape[0]
    flat_qkv = qkv_weight.reshape(model_width, 3 * qkv_weight.shape[2])

    def project(patch_block):
        normed_tok = embed_norm(patch_block, flat_patch)
        return jnp.dot(normed_tok, flat_qkv, preferred_element_type=jnp.float32).astype(jnp.bfloat16)
    projected = lax.map(project, patches)
    return projected.reshape(-1, 3, qkv_weight.shape[2])
```

```python
import jax
import jax.numpy as jnp
from jax import lax
from jax.sharding import PartitionSpec as P


def passed_along(block, axis, distance):
    devices = range(lax.axis_size(axis))
    route = [(i - distance, i) for i in devices if i - distance in devices]
    return lax.ppermute(block, axis, route)


def padded_2(block, sides, width):
    for axis, dim in sides:
        count = lax.axis_size(axis)
        forward = [(i, i + 1) for i in range(count - 1)]
        backward = [(target, source) for source, target in forward]
        low = lax.ppermute(
            lax.slice_in_dim(block, block.shape[dim] - width, None, axis=dim), axis, forward
        )
        high = lax.ppermute(lax.slice_in_dim(block, 0, width, axis=dim), axis, backward)
        block = jnp.concatenate([low, block, high], axis=dim)
    return block


def rms_silu(tensor_in):
    values = tensor_in.astype(jnp.float32)
    scaled = values * lax.rsqrt(jnp.mean(values * values, axis=-1, keepdims=True) + 1e-06)
    return jax.nn.silu(scaled).astype(jnp.bfloat16)


def shifted_history(current, cache_frames):
    position = lax.axis_index("tm")
    earlier = passed_along(current, "tm", 1)
    earlier = jnp.where(position == 0, cache_frames[1:2], earlier)
    earliest = passed_along(earlier, "tm", 1)
    earliest = jnp.where(position == 0, cache_frames[0:1], earliest)
    return (earliest, earlier)


def neighbourhood(current, cache_frames):
    earliest, earlier = shifted_history(current, cache_frames)
    stacked = jnp.concatenate([earliest, earlier, current], axis=0)
    window_stack = padded_2(stacked, (("rows", 1),), 1)
    return window_stack


def causal_conv(window_stack, kernel):
    padded = jnp.pad(window_stack, ((0, 0), (0, 0), (1, 1), (0, 0)))
    row_count = window_stack.shape[1] - 2
    col_count = window_stack.shape[2]
    tap_list = []
    for tap_time in range(3):
        for tap_row in range(3):
            for tap_col in range(3):
                tap_list.append(
                    padded[
                        tap_time, tap_row : tap_row + row_count, tap_col : tap_col + col_count, :
                    ]
                )
    columns = jnp.concatenate(tap_list, axis=-1)
    flat_kernel = kernel.reshape(-1, kernel.shape[-1])
    return jnp.dot(columns, flat_kernel, preferred_element_type=jnp.float32)


def rounded(values):
    return lax.reduce_precision(values, 8, 7)


def three_parts(values):
    first = rounded(values)
    second = rounded(values - first)
    third = values - first - second
    return [part.astype(jnp.bfloat16) for part in (first, second, third)]


def folded_weights(flat_patch, flat_qkv):
    weights = flat_patch.astype(jnp.float32)
    depth, width = weights.shape
    centred = weights - jnp.mean(weights, axis=1, keepdims=True)
    parts = jnp.concatenate(three_parts(centred), axis=0)
    left = jnp.concatenate([flat_qkv, parts], axis=0)
    product = lax.dot_general(left, parts, (((1,), (1,)), ((), ())), preferred_element_type=jnp.float32)
    product = product[:, :depth] + product[:, depth : 2 * depth] + product[:, 2 * depth :]
    split = flat_qkv.shape[0]
    gram = product[split:]
    gram = (gram[:depth] + gram[depth : 2 * depth] + gram[2 * depth :]) / width
    return jnp.concatenate([product[:split], gram], axis=0)


def local(features, conv_cache, head_cache, conv_weight, head_weight, patch_weight, qkv_weight):
    normed_in = rms_silu(features)
    update = causal_conv(neighbourhood(normed_in, conv_cache), conv_weight)
    residual = (features[0].astype(jnp.float32) + update).astype(jnp.bfloat16)
    normed_out = rms_silu(residual)[None]
    latents = causal_conv(neighbourhood(normed_out, head_cache), head_weight).astype(jnp.bfloat16)
    row_count, col_count, latent_dim = latents.shape
    depth = 4 * latent_dim
    local_cols = qkv_weight.shape[2]
    patches = latents.reshape(row_count // 2, 2, col_count // 2, 2, latent_dim)
    patches = patches.transpose(1, 3, 4, 0, 2).reshape(depth, -1)
    tokens = patches.shape[1]
    blocks = lax.axis_size("rows")
    gathered = lax.all_to_all(
        jnp.broadcast_to(patches[None], (blocks, depth, tokens)), "rows", 0, 0, tiled=True
    )
    patch_cols = gathered.transpose(1, 0, 2).reshape(depth, blocks * tokens)
    flat_qkv = qkv_weight.transpose(1, 2, 0).reshape(3 * local_cols, -1)
    folded = folded_weights(patch_weight.reshape(depth, -1), flat_qkv)
    left = jnp.concatenate(three_parts(folded), axis=1)
    right = jnp.concatenate([patch_cols] * 3, axis=0)
    product = jnp.dot(left, right, preferred_element_type=jnp.float32)
    variance = jnp.sum(product[3 * local_cols :] * patch_cols.astype(jnp.float32), axis=0)
    scale = lax.rsqrt(jnp.maximum(variance, 0.0) + 1e-06)
    result = (product[: 3 * local_cols] * scale[None]).astype(jnp.bfloat16)
    return result.reshape(3, local_cols, blocks * tokens).transpose(2, 0, 1)


def solution(mesh):
    return jax.shard_map(
        local,
        mesh=mesh,
        in_specs=(
            P("tm", "rows", None, None),
            P(None, "rows", None, None),
            P(None, "rows", None, None),
            P(),
            P(),
            P(),
            P(None, None, "rows"),
        ),
        out_specs=P("tm", None, "rows"),
        check_vma=False,
    )
```

```python
import functools

import jax
import jax.numpy as jnp
from jax import lax
from jax.experimental import pallas as pl
from jax.experimental.pallas import tpu as pltpu
from jax.sharding import PartitionSpec as P

F32 = jnp.float32
BF16 = jnp.bfloat16
EPS = 1e-06
STEP = 14
WIN = 16

MEMORY = 56 << 20


def iota(shape, axis):
    return lax.broadcasted_iota(jnp.int32, shape, axis)


def rms_silu(values):
    scaled = values * lax.rsqrt(jnp.mean(values * values, axis=-1, keepdims=True) + EPS)
    return scaled / (1.0 + jnp.exp(-scaled))


def three_parts(values):
    first = values.astype(BF16)
    rest = values - first.astype(F32)
    second = rest.astype(BF16)
    third = (rest - second.astype(F32)).astype(BF16)
    return first, second, third


def rows_times_rows(left, right):
    return lax.dot_general(left, right, (((1,), (1,)), ((), ())), preferred_element_type=F32)


def feature_windows_kernel(groups, features, send):
    rows, cols, _ = features.shape
    shape = (groups * WIN, cols)
    place = iota(shape, 0)
    source = STEP * (place // WIN) + place % WIN - 1
    pick = (iota(shape, 1) == source).astype(BF16)
    for row in range(rows):
        picked = jnp.dot(pick, features[row], preferred_element_type=F32).astype(BF16)
        for group in range(groups):
            send[group, row] = picked[group * WIN : (group + 1) * WIN]


def cache_windows_kernel(position, conv_cache, head_cache, conv_win, head_win):
    frames, rows, cols, _ = conv_cache.shape
    shape = (WIN, cols)
    place = iota(shape, 0)
    first = STEP * position[0]
    pick_conv = (iota(shape, 1) == first + place - 1).astype(BF16)
    pick_head = ((iota(shape, 1) == first + place) & (place < STEP)).astype(BF16)
    for frame in range(frames):
        for row in range(rows):
            conv_win[frame, row] = jnp.dot(
                pick_conv, conv_cache[frame, row], preferred_element_type=F32
            ).astype(BF16)
            head_win[frame, row] = jnp.dot(
                pick_head, head_cache[frame, row], preferred_element_type=F32
            ).astype(BF16)


def section_kernel(
    cols, position, main, low, high, conv_win, head_win, weight, head, out, normed, sums, left, head_rows, hidden
):
    frames, rows, win, width = main.shape
    count = frames * rows * win
    tap = pl.program_id(0)

    @pl.when(tap == 0)
    def _():
        normed[0:2, 1 : rows + 1] = conv_win[...]
        normed[0:2, 0] = low[0:2]
        normed[0:2, rows + 1] = high[0:2]
        normed[2:, 1 : rows + 1] = rms_silu(main[...].astype(F32)).astype(BF16)
        normed[2:, 0] = rms_silu(low[2:].astype(F32)).astype(BF16)
        normed[2:, rows + 1] = rms_silu(high[2:].astype(F32)).astype(BF16)

    for b in range(3):
        left[:, b * width : (b + 1) * width] = normed[pl.ds(tap, frames), b : b + rows].reshape(
            count, width
        )
    for c in range(3):
        product = jnp.dot(
            left[...], weight[0, :, c].reshape(3 * width, width), preferred_element_type=F32
        )

        @pl.when(tap == 0)
        def _():
            sums[c] = product

        @pl.when(tap > 0)
        def _():
            sums[c] += product

    @pl.when(tap == 2)
    def _():
        update = sums[0] + pltpu.roll(sums[1], count - 1, 0) + pltpu.roll(sums[2], count - 2, 0)
        own = pltpu.roll(main[...].astype(F32).reshape(count, width), count - 1, 0)
        residual = (own + update).astype(BF16).astype(F32)
        place = iota((count, 1), 0) % win
        inside = (place < STEP) & (STEP * position[0] + place < cols)
        normed_out = jnp.where(inside, rms_silu(residual), 0.0).astype(BF16)
        hidden[0 : 2 * rows * win] = head_win[...].reshape(2 * rows * win, width)
        hidden[2 * rows * win :] = normed_out
        depth = head.shape[3]
        head_rows[...] = jnp.zeros_like(head_rows)
        for a in range(3):
            for b in range(3):
                for c in range(3):
                    start = (3 * a + c) * 128 + (2 - b) * depth
                    head_rows[start : start + depth] = head[a, b, c]
        taps = rows_times_rows(hidden[...], head_rows[...])
        shifted = []
        for c in range(3):
            total = jnp.zeros((count, 128), F32)
            for a in range(3):
                total += taps[
                    a * rows * win : a * rows * win + count, (3 * a + c) * 128 : (3 * a + c + 1) * 128
                ]
            shifted.append(total if c == 2 else pltpu.roll(total, 2 - c, 0))
        total = (shifted[0] + shifted[1] + shifted[2]).reshape(frames, rows, win, 128)
        for frame in range(frames):
            piece = total[frame, 0]
            for row in range(1, rows):
                piece += pltpu.roll(total[frame, row], depth * row, 1)
            piece = piece.astype(BF16)
            for target in range(out.shape[1]):
                out[frame, target] = piece


def folded_kernel(patch, qkv, folded, gram, parts):
    depth = patch.shape[2]
    width = patch.shape[3]
    positions = 4 * depth

    def stacked(values):
        pieces = list(three_parts(values))
        pieces.append(jnp.zeros_like(pieces[0]))
        return jnp.concatenate(pieces, axis=1)

    @pl.when(pl.program_id(0) == 0)
    def _():
        for b in range(2):
            for a in range(2):
                weights = patch[a, b].astype(F32)
                centred = weights - jnp.mean(weights, axis=1, keepdims=True)
                for index, part in enumerate(three_parts(centred)):
                    start = index * positions + (2 * b + a) * depth
                    parts[start : start + depth] = part
        product = rows_times_rows(parts[...], parts[...])
        total = jnp.zeros((positions, positions), F32)
        for i in range(3):
            for k in range(3):
                total += product[
                    i * positions : (i + 1) * positions, k * positions : (k + 1) * positions
                ]
        gram[...] = stacked(total / width)

    product = rows_times_rows(qkv[...], parts[...])
    total = (
        product[:, :positions] + product[:, positions : 2 * positions] + product[:, 2 * positions :]
    )
    folded[...] = stacked(total)


def project_kernel(depth, pieces, folded, gram, out, sums, patches, scale):
    groups, blocks, win, lanes = pieces.shape
    positions = 4 * depth
    tokens = patches.shape[0]
    half = tokens // (2 * blocks)
    pad = (half + 7) // 8 * 8

    @pl.when(pl.program_id(0) == 0)
    def _():
        shape = (2 * pad, groups * win)
        row = iota(shape, 0)
        place = iota(shape, 1)
        odd = (row >= pad).astype(jnp.int32)
        patch_col = row - pad * odd
        column = STEP * (place // win) + place % win - 1
        pick = ((column == 2 * patch_col + odd) & (patch_col < half)).astype(BF16)
        for block in range(blocks):
            source = pieces[:, block].reshape(groups * win, lanes)
            sums[block] = jnp.dot(pick, source, preferred_element_type=F32)
        slot = iota((1, lanes), 1) // depth
        for block in range(blocks):
            total = sums[block]
            if block > 0:
                total += jnp.where(slot == 1, pltpu.roll(sums[block - 1], 4 * depth, 1), 0.0)
            if block < blocks - 1:
                total += jnp.where(slot == 4, pltpu.roll(sums[block + 1], 4 * depth, 1), 0.0)
            for i in range(2):
                start = (1 + 2 * i) * depth
                even = pltpu.roll(total, lanes - start, 1)[0:half]
                uneven = pltpu.roll(total, (lanes + 2 * depth - start) % lanes, 1)[pad : pad + half]
                patch = jnp.where(slot < 2, even, jnp.where(slot < 4, uneven, 0.0))
                patch = patch + pltpu.roll(patch, positions, 1)
                first = (2 * block + i) * half
                patches[first : first + half] = patch
        rounded = patches[...].astype(BF16)
        both = jnp.concatenate([rounded, rounded], axis=1)
        same = iota((positions, 2 * lanes), 0) == iota((positions, 2 * lanes), 1)
        probe = jnp.concatenate([gram[...], same.astype(BF16)], axis=0)
        product = rows_times_rows(probe, both)
        variance = jnp.sum(product[:positions] * product[positions:], axis=0, keepdims=True)
        scale[...] = lax.rsqrt(jnp.maximum(variance, 0.0) + EPS)

    rounded = patches[...].astype(BF16)
    both = jnp.concatenate([rounded, rounded], axis=1)
    out[...] = (rows_times_rows(folded[...], both) * scale[...]).astype(BF16)


def params(**kwargs):
    return pltpu.CompilerParams(vmem_limit_bytes=MEMORY, **kwargs)


def whole(shape):
    return pl.BlockSpec(shape, lambda *_: (0,) * len(shape))


def local(features, conv_cache, head_cache, conv_weight, head_weight, patch_weight, qkv_weight):
    groups = lax.axis_size("tm")
    blocks = lax.axis_size("rows")
    _, rows, cols, width = features.shape
    frames = groups
    depth = head_weight.shape[-1]
    local_cols = qkv_weight.shape[2]
    model = qkv_weight.shape[0]
    tokens = blocks * rows * cols // 4
    position = lax.axis_index("tm").astype(jnp.int32).reshape(1)
    scalar = pl.BlockSpec(memory_space=pltpu.SMEM)

    send = pl.pallas_call(
        functools.partial(feature_windows_kernel, groups),
        out_shape=jax.ShapeDtypeStruct((groups, rows, WIN, width), BF16),
        compiler_params=params(),
        name="feature_windows",
    )(features[0])
    main = lax.all_to_all(send, "tm", 0, 0, tiled=True)

    conv_win, head_win = pl.pallas_call(
        cache_windows_kernel,
        in_specs=[scalar, whole(conv_cache.shape), whole(head_cache.shape)],
        out_specs=[whole((2, rows, WIN, width))] * 2,
        grid=(1,),
        out_shape=[jax.ShapeDtypeStruct((2, rows, WIN, width), BF16)] * 2,
        compiler_params=params(),
        name="cache_windows",
    )(position, conv_cache, head_cache)

    flat_qkv = qkv_weight.transpose(1, 2, 0).reshape(3 * local_cols, model)
    positions = 4 * depth
    steps = 4
    share = 3 * local_cols // steps
    folded, gram = pl.pallas_call(
        folded_kernel,
        grid=(steps,),
        in_specs=[whole(patch_weight.shape), pl.BlockSpec((share, model), lambda i: (i, 0))],
        out_specs=[
            pl.BlockSpec((share, 4 * positions), lambda i: (i, 0)),
            whole((positions, 4 * positions)),
        ],
        out_shape=[
            jax.ShapeDtypeStruct((3 * local_cols, 4 * positions), BF16),
            jax.ShapeDtypeStruct((positions, 4 * positions), BF16),
        ],
        scratch_shapes=[pltpu.VMEM((3 * positions, model), BF16)],
        compiler_params=params(),
        name="folded_weights",
    )(patch_weight, flat_qkv)

    down = [(i, i + 1) for i in range(blocks - 1)]
    up = [(i + 1, i) for i in range(blocks - 1)]
    low = lax.ppermute(jnp.concatenate([conv_win[:, rows - 1], main[:, rows - 1]]), "rows", down)
    high = lax.ppermute(jnp.concatenate([conv_win[:, 0], main[:, 0]]), "rows", up)

    head = head_weight.transpose(0, 1, 2, 4, 3)
    count = frames * rows * WIN
    partial = pl.pallas_call(
        functools.partial(section_kernel, cols),
        grid=(3,),
        in_specs=[
            scalar,
            whole(main.shape),
            whole(low.shape),
            whole(high.shape),
            whole(conv_win.shape),
            whole(head_win.shape),
            pl.BlockSpec((1, 3, 3, width, width), lambda i: (i, 0, 0, 0, 0)),
            whole(head.shape),
        ],
        out_specs=whole((frames, blocks, WIN, 128)),
        out_shape=jax.ShapeDtypeStruct((frames, blocks, WIN, 128), BF16),
        scratch_shapes=[
            pltpu.VMEM((frames + 2, rows + 2, WIN, width), BF16),
            pltpu.VMEM((3, count, width), F32),
            pltpu.VMEM((count, 3 * width), BF16),
            pltpu.VMEM((9 * 128, width), BF16),
            pltpu.VMEM((count + 2 * rows * WIN, width), BF16),
        ],
        compiler_params=params(),
        name="section",
    )(position, main, low, high, conv_win, head_win, conv_weight, head)

    pieces = lax.all_to_all(
        partial.reshape(frames * blocks, WIN, 128), ("tm", "rows"), 0, 0, tiled=True
    ).reshape(groups, blocks, WIN, 128)

    half = cols // 2
    pad = (half + 7) // 8 * 8
    result = pl.pallas_call(
        functools.partial(project_kernel, depth),
        grid=(steps,),
        in_specs=[
            whole(pieces.shape),
            pl.BlockSpec((share, 4 * positions), lambda i: (i, 0)),
            whole((positions, 4 * positions)),
        ],
        out_specs=pl.BlockSpec((share, tokens), lambda i: (i, 0)),
        out_shape=jax.ShapeDtypeStruct((3 * local_cols, tokens), BF16),
        scratch_shapes=[
            pltpu.VMEM((blocks, 2 * pad, 128), F32),
            pltpu.VMEM((tokens, 128), F32),
            pltpu.VMEM((1, tokens), F32),
        ],
        compiler_params=params(),
        name="project",
    )(pieces, folded, gram)
    return result.reshape(3, local_cols, tokens).transpose(2, 0, 1)


def solution(mesh):
    return jax.shard_map(
        local,
        mesh=mesh,
        in_specs=(
            P("tm", "rows", None, None),
            P(None, "rows", None, None),
            P(None, "rows", None, None),
            P(),
            P(),
            P(),
            P(None, None, "rows"),
        ),
        out_specs=P("tm", None, "rows"),
        check_vma=False,
    )
```

```python
import functools

import jax
import jax.numpy as jnp
from jax import lax
from jax.experimental import pallas as pl
from jax.experimental.pallas import tpu as pltpu
from jax.sharding import PartitionSpec as P

F32 = jnp.float32
BF16 = jnp.bfloat16
EPS = 1e-06
STEP = 14
WIN = 16


def iota(shape, axis):
    return lax.broadcasted_iota(jnp.int32, shape, axis)


def rms_silu(values):
    scaled = values * lax.rsqrt(jnp.mean(values * values, axis=-1, keepdims=True) + EPS)
    return scaled / (1.0 + jnp.exp(-scaled))


def three_parts(values):
    first = values.astype(BF16)
    rest = values - first.astype(F32)
    second = rest.astype(BF16)
    third = (rest - second.astype(F32)).astype(BF16)
    return first, second, third


def rows_times_rows(left, right):
    return lax.dot_general(left, right, (((1,), (1,)), ((), ())), preferred_element_type=F32)


def feature_windows_kernel(groups, features, send, rows_in, sems):
    rows, cols, _ = features.shape
    copies = [
        pltpu.make_async_copy(features.at[row], rows_in.at[row], sems.at[row]) for row in range(rows)
    ]
    for copy in copies:
        copy.start()
    shape = (groups * WIN, cols)
    place = iota(shape, 0)
    source = STEP * (place // WIN) + place % WIN - 1
    pick = (iota(shape, 1) == source).astype(BF16)
    for row in range(rows):
        copies[row].wait()
        picked = jnp.dot(pick, rows_in[row], preferred_element_type=F32).astype(BF16)
        for group in range(groups):
            send[group, row] = picked[group * WIN : (group + 1) * WIN]


def cache_windows_kernel(position, conv_cache, head_cache, conv_win, head_win, conv_in, head_in, sems):
    frames, rows, cols, _ = conv_cache.shape
    copies = [
        pltpu.make_async_copy(conv_cache, conv_in, sems.at[0]),
        pltpu.make_async_copy(head_cache, head_in, sems.at[1]),
    ]
    for copy in copies:
        copy.start()
    shape = (WIN, cols)
    place = iota(shape, 0)
    first = STEP * position[0]
    pick_conv = (iota(shape, 1) == first + place - 1).astype(BF16)
    pick_head = ((iota(shape, 1) == first + place) & (place < STEP)).astype(BF16)
    for copy, pick, source, out in (
        (copies[0], pick_conv, conv_in, conv_win),
        (copies[1], pick_head, head_in, head_win),
    ):
        copy.wait()
        for frame in range(frames):
            for row in range(rows):
                out[frame, row] = jnp.dot(
                    pick, source[frame, row], preferred_element_type=F32
                ).astype(BF16)


def weights_kernel(after, weight, head, weight_out, head_rows, head_in, sems):
    depth = head.shape[3]
    copies = [pltpu.make_async_copy(head, head_in, sems.at[3])]
    copies += [pltpu.make_async_copy(weight.at[a], weight_out.at[a], sems.at[a]) for a in range(3)]
    for copy in copies:
        copy.start()
    head_rows[...] = jnp.zeros_like(head_rows)
    copies[0].wait()
    for a in range(3):
        for b in range(3):
            for c in range(3):
                start = (3 * a + c) * 128 + (2 - b) * depth
                head_rows[start : start + depth] = head_in[a, b, c]
    for copy in copies[1:]:
        copy.wait()


def section_kernel(
    cols, depth, position, main, low, high, conv_win, head_win, weight, head_rows, out, normed, hidden
):
    frames, rows, win, width = main.shape
    count = frames * rows * win
    normed[0:2, 1 : rows + 1] = conv_win[...]
    normed[0:2, 0] = low[0:2]
    normed[0:2, rows + 1] = high[0:2]
    normed[2:, 1 : rows + 1] = rms_silu(main[...].astype(F32)).astype(BF16)
    normed[2:, 0] = rms_silu(low[2:].astype(F32)).astype(BF16)
    normed[2:, rows + 1] = rms_silu(high[2:].astype(F32)).astype(BF16)
    before = 2 * rows * win
    hidden[0:before] = head_win[...].reshape(before, width)

    together = 4
    chunk = together * rows * win
    place = iota((chunk, 1), 0) % win
    inside = (place < STEP) & (STEP * position[0] + place < cols)
    for first in range(0, frames, together):
        left = jnp.concatenate(
            [
                normed[first + a : first + a + together, b : b + rows].reshape(chunk, width)
                for a in range(3)
                for b in range(3)
            ],
            axis=1,
        )
        right = jnp.concatenate(
            [weight[:, :, c].reshape(9 * width, width) for c in range(3)], axis=1
        )
        sums = jnp.dot(left, right, preferred_element_type=F32)
        update = (
            sums[:, :width]
            + pltpu.roll(sums[:, width : 2 * width], chunk - 1, 0)
            + pltpu.roll(sums[:, 2 * width :], chunk - 2, 0)
        )
        own = main[first : first + together].astype(F32).reshape(chunk, width)
        residual = (pltpu.roll(own, chunk - 1, 0) + update).astype(BF16).astype(F32)
        start = before + first * rows * win
        hidden[start : start + chunk] = jnp.where(inside, rms_silu(residual), 0.0).astype(BF16)

    taps = rows_times_rows(hidden[...], head_rows[...])
    shifted = []
    for c in range(3):
        total = jnp.zeros((count, 128), F32)
        for a in range(3):
            total += taps[
                a * rows * win : a * rows * win + count, (3 * a + c) * 128 : (3 * a + c + 1) * 128
            ]
        shifted.append(total if c == 2 else pltpu.roll(total, 2 - c, 0))
    total = (shifted[0] + shifted[1] + shifted[2]).reshape(frames, rows, win, 128)
    for frame in range(frames):
        piece = total[frame, 0]
        for row in range(1, rows):
            piece += pltpu.roll(total[frame, row], depth * row, 1)
        piece = piece.astype(BF16)
        for target in range(out.shape[1]):
            out[frame, target] = piece


def folded_kernel(patch, qkv, folded, gram, parts, qkv_in, sems):
    depth = patch.shape[2]
    width = patch.shape[3]
    positions = 4 * depth
    chunks = sems.shape[0]
    share = qkv.shape[0] // chunks
    copies = []
    for index in range(chunks):
        part = pl.ds(index * share, share)
        copies.append(pltpu.make_async_copy(qkv.at[part], qkv_in.at[part], sems.at[index]))
        copies[-1].start()

    def stacked(values):
        pieces = list(three_parts(values))
        pieces.append(jnp.zeros_like(pieces[0]))
        return jnp.concatenate(pieces, axis=1)

    for b in range(2):
        for a in range(2):
            weights = patch[a, b].astype(F32)
            centred = weights - jnp.mean(weights, axis=1, keepdims=True)
            for index, part in enumerate(three_parts(centred)):
                start = index * positions + (2 * b + a) * depth
                parts[start : start + depth] = part
    product = rows_times_rows(parts[...], parts[...])
    total = jnp.zeros((positions, positions), F32)
    for i in range(3):
        for k in range(3):
            total += product[
                i * positions : (i + 1) * positions, k * positions : (k + 1) * positions
            ]
    gram[...] = stacked(total / width)

    for index in range(chunks):
        copies[index].wait()
        part = pl.ds(index * share, share)
        product = rows_times_rows(qkv_in[part], parts[...])
        folded[part] = stacked(
            product[:, :positions]
            + product[:, positions : 2 * positions]
            + product[:, 2 * positions :]
        )


def project_kernel(depth, pieces, folded, gram, out, sums, patches, columns, staged, sems):
    groups, blocks, win, lanes = pieces.shape
    positions = 4 * depth
    tokens = patches.shape[0]
    half = tokens // (2 * blocks)
    pad = (half + 7) // 8 * 8

    shape = (2 * pad, groups * win)
    row = iota(shape, 0)
    place = iota(shape, 1)
    odd = (row >= pad).astype(jnp.int32)
    patch_col = row - pad * odd
    column = STEP * (place // win) + place % win - 1
    pick = ((column == 2 * patch_col + odd) & (patch_col < half)).astype(BF16)
    for block in range(blocks):
        source = pieces[:, block].reshape(groups * win, lanes)
        sums[block] = jnp.dot(pick, source, preferred_element_type=F32)
    slot = iota((1, lanes), 1) // depth
    turned = [None] * blocks
    for block in range(blocks):
        for near in (block, block + 1):
            if near < blocks and turned[near] is None:
                turned[near] = pltpu.roll(sums[near], 4 * depth, 1)
        total = sums[block]
        if block > 0:
            total += jnp.where(slot == 1, turned[block - 1], 0.0)
        if block < blocks - 1:
            total += jnp.where(slot == 4, turned[block + 1], 0.0)
        for i in range(2):
            start = (1 + 2 * i) * depth
            even = pltpu.roll(total[0:pad], lanes - start, 1)
            uneven = pltpu.roll(total[pad:], (lanes + 2 * depth - start) % lanes, 1)
            patch = jnp.where(slot < 2, even, jnp.where(slot < 4, uneven, 0.0))
            first = (2 * block + i) * half
            patches[first : first + half] = patch[0:half]
    turned = jnp.transpose(patches[...])[0:positions]
    rounded = turned.astype(BF16)
    for index in range(4):
        columns[index * positions : (index + 1) * positions] = rounded
    product = jnp.dot(gram[...], columns[...], preferred_element_type=F32)
    variance = jnp.sum(product * rounded.astype(F32), axis=0, keepdims=True)
    scale = lax.rsqrt(jnp.maximum(variance, 0.0) + EPS)
    chunks = sems.shape[0]
    share = folded.shape[0] // chunks
    copies = []
    for index in range(chunks):
        part = pl.ds(index * share, share)
        product = jnp.dot(folded[part], columns[...], preferred_element_type=F32)
        staged[part] = (product * scale).astype(BF16)
        copies.append(pltpu.make_async_copy(staged.at[part], out.at[part], sems.at[index]))
        copies[-1].start()
    for copy in copies:
        copy.wait()


ON_CHIP = pl.BlockSpec(memory_space=pltpu.VMEM)
IN_HBM = pl.BlockSpec(memory_space=pltpu.HBM)
SCALAR = pl.BlockSpec(memory_space=pltpu.SMEM)


def params(mebibytes):
    return pltpu.CompilerParams(vmem_limit_bytes=mebibytes << 20)


def in_hbm(array):
    return pltpu.with_memory_space_constraint(array, pltpu.HBM)


def feature_windows(features, groups):
    rows, cols, width = features.shape
    return pl.pallas_call(
        functools.partial(feature_windows_kernel, groups),
        in_specs=[IN_HBM],
        out_specs=ON_CHIP,
        out_shape=pltpu.VMEM((groups, rows, WIN, width), BF16),
        scratch_shapes=[pltpu.VMEM(features.shape, BF16), pltpu.SemaphoreType.DMA((rows,))],
        compiler_params=params(8),
        name="feature_windows",
    )(in_hbm(features))


def cache_windows(position, conv_cache, head_cache):
    frames, rows, cols, width = conv_cache.shape
    window = pltpu.VMEM((frames, rows, WIN, width), BF16)
    return pl.pallas_call(
        cache_windows_kernel,
        in_specs=[SCALAR, IN_HBM, IN_HBM],
        out_specs=[ON_CHIP] * 2,
        out_shape=[window, window],
        scratch_shapes=[
            pltpu.VMEM(conv_cache.shape, BF16),
            pltpu.VMEM(head_cache.shape, BF16),
            pltpu.SemaphoreType.DMA((2,)),
        ],
        compiler_params=params(8),
        name="cache_windows",
    )(position, in_hbm(conv_cache), in_hbm(head_cache))


def weights_on_chip(after, weight, head):
    return pl.pallas_call(
        weights_kernel,
        in_specs=[ON_CHIP, IN_HBM, IN_HBM],
        out_specs=[ON_CHIP] * 2,
        out_shape=[pltpu.VMEM(weight.shape, BF16), pltpu.VMEM((9 * 128, weight.shape[3]), BF16)],
        scratch_shapes=[pltpu.VMEM(head.shape, BF16), pltpu.SemaphoreType.DMA((4,))],
        compiler_params=params(8),
        name="weights_on_chip",
    )(after, in_hbm(weight), in_hbm(head))


def section(position, main, low, high, conv_win, head_win, weight, head_rows, cols, depth, blocks):
    frames, rows, win, width = main.shape
    return pl.pallas_call(
        functools.partial(section_kernel, cols, depth),
        in_specs=[SCALAR] + [ON_CHIP] * 7,
        out_specs=ON_CHIP,
        out_shape=pltpu.VMEM((frames, blocks, win, 128), BF16),
        scratch_shapes=[
            pltpu.VMEM((frames + 2, rows + 2, win, width), BF16),
            pltpu.VMEM(((frames + 2) * rows * win, width), BF16),
        ],
        compiler_params=params(20),
        name="section",
    )(position, main, low, high, conv_win, head_win, weight, head_rows)


def folded_weights(patch, qkv):
    positions = 4 * patch.shape[2]
    chunks = 4
    return pl.pallas_call(
        folded_kernel,
        in_specs=[ON_CHIP, IN_HBM],
        out_specs=[ON_CHIP] * 2,
        out_shape=[
            pltpu.VMEM((qkv.shape[0], 4 * positions), BF16),
            pltpu.VMEM((positions, 4 * positions), BF16),
        ],
        scratch_shapes=[
            pltpu.VMEM((3 * positions, patch.shape[3]), BF16),
            pltpu.VMEM(qkv.shape, BF16),
            pltpu.SemaphoreType.DMA((chunks,)),
        ],
        compiler_params=params(24),
        name="folded_weights",
    )(patch, in_hbm(qkv))


def project(pieces, folded, gram, cols, depth):
    groups, blocks, win, lanes = pieces.shape
    half = cols // 2
    pad = (half + 7) // 8 * 8
    tokens = 2 * blocks * half
    outputs = folded.shape[0]
    chunks = 4
    return pl.pallas_call(
        functools.partial(project_kernel, depth),
        in_specs=[ON_CHIP] * 3,
        out_specs=IN_HBM,
        out_shape=pltpu.HBM((outputs, tokens), BF16),
        scratch_shapes=[
            pltpu.VMEM((blocks, 2 * pad, lanes), F32),
            pltpu.VMEM((tokens, lanes), F32),
            pltpu.VMEM((16 * depth, tokens), BF16),
            pltpu.VMEM((outputs, tokens), BF16),
            pltpu.SemaphoreType.DMA((chunks,)),
        ],
        compiler_params=params(20),
        name="project",
    )(pieces, folded, gram)


def local(features, conv_cache, head_cache, conv_weight, head_weight, patch_weight, qkv_weight):
    groups = lax.axis_size("tm")
    blocks = lax.axis_size("rows")
    _, rows, cols, width = features.shape
    depth = head_weight.shape[-1]
    local_cols = qkv_weight.shape[2]
    position = lax.axis_index("tm").astype(jnp.int32).reshape(1)
    head = head_weight.transpose(0, 1, 2, 4, 3)
    flat_qkv = qkv_weight.transpose(1, 2, 0).reshape(3 * local_cols, qkv_weight.shape[0])

    main = lax.all_to_all(feature_windows(features[0], groups), "tm", 0, 0, tiled=True)
    conv_win, head_win = cache_windows(position, conv_cache, head_cache)
    down = [(i, i + 1) for i in range(blocks - 1)]
    up = [(i + 1, i) for i in range(blocks - 1)]
    low = lax.ppermute(jnp.concatenate([conv_win[:, rows - 1], main[:, rows - 1]]), "rows", down)
    high = lax.ppermute(jnp.concatenate([conv_win[:, 0], main[:, 0]]), "rows", up)
    weight, head_rows = weights_on_chip(main, conv_weight, head)
    partial = section(
        position, main, low, high, conv_win, head_win, weight, head_rows, cols, depth, blocks
    )
    pieces = lax.all_to_all(
        partial.reshape(groups * blocks, WIN, 128), ("tm", "rows"), 0, 0, tiled=True
    ).reshape(groups, blocks, WIN, 128)
    folded, gram = folded_weights(patch_weight, flat_qkv)
    result = project(pieces, folded, gram, cols, depth)
    return result.reshape(3, local_cols, result.shape[1]).transpose(2, 0, 1)


def solution(mesh):
    return jax.shard_map(
        local,
        mesh=mesh,
        in_specs=(
            P("tm", "rows", None, None),
            P(None, "rows", None, None),
            P(None, "rows", None, None),
            P(),
            P(),
            P(),
            P(None, None, "rows"),
        ),
        out_specs=P("tm", None, "rows"),
        check_vma=False,
    )
```

```python
import functools

import jax
import jax.numpy as jnp
from jax import lax
from jax.experimental import pallas as pl
from jax.experimental.pallas import tpu as pltpu
from jax.sharding import PartitionSpec as P

F32 = jnp.float32
BF16 = jnp.bfloat16
EPS = 1e-06
STEP = 14
WIN = 16


def iota(shape, axis):
    return lax.broadcasted_iota(jnp.int32, shape, axis)


def rms_silu(values):
    scaled = values * lax.rsqrt(jnp.mean(values * values, axis=-1, keepdims=True) + EPS)
    return scaled / (1.0 + jnp.exp(-scaled))


def three_parts(values):
    first = values.astype(BF16)
    rest = values - first.astype(F32)
    second = rest.astype(BF16)
    third = (rest - second.astype(F32)).astype(BF16)
    return first, second, third


def rows_times_rows(left, right):
    return lax.dot_general(left, right, (((1,), (1,)), ((), ())), preferred_element_type=F32)


def feature_windows_kernel(groups, features, send, rows_in, windows, sems_in, sems_out):
    rows, cols, width = features.shape
    copies = [
        pltpu.make_async_copy(features.at[row], rows_in.at[row], sems_in.at[row])
        for row in range(rows)
    ]
    for copy in copies:
        copy.start()
    after = STEP * (groups - 1) + WIN - 1 - cols
    results = []
    for row in range(rows):
        copies[row].wait()
        values = jnp.concatenate(
            [
                jnp.zeros((8, width), F32),
                rows_in[row].astype(F32),
                jnp.zeros(((after + 7) // 8 * 8, width), F32),
            ],
            axis=0,
        )
        for group in range(groups):
            first = 8 + STEP * group - 1
            windows[group, row] = values[first : first + WIN].astype(BF16)
        part = pl.ds(row, 1)
        results.append(
            pltpu.make_async_copy(windows.at[:, part], send.at[:, part], sems_out.at[row])
        )
        results[-1].start()
    for copy in results:
        copy.wait()


def cache_windows_kernel(position, conv_cache, head_cache, conv_win, head_win, conv_in, head_in, sems):
    frames, rows, cols, _ = conv_cache.shape
    copies = [
        pltpu.make_async_copy(conv_cache, conv_in, sems.at[0]),
        pltpu.make_async_copy(head_cache, head_in, sems.at[1]),
    ]
    for copy in copies:
        copy.start()
    shape = (WIN, cols)
    place = iota(shape, 0)
    first = STEP * position[0]
    pick_conv = (iota(shape, 1) == first + place - 1).astype(BF16)
    pick_head = ((iota(shape, 1) == first + place) & (place < STEP)).astype(BF16)
    for copy, pick, source, out in (
        (copies[0], pick_conv, conv_in, conv_win),
        (copies[1], pick_head, head_in, head_win),
    ):
        copy.wait()
        for frame in range(frames):
            for row in range(rows):
                out[frame, row] = jnp.dot(
                    pick, source[frame, row], preferred_element_type=F32
                ).astype(BF16)


def weights_kernel(main, weight, head, weight_out, head_rows, normed, head_in, sems):
    depth = head.shape[3]
    copies = [pltpu.make_async_copy(head, head_in, sems.at[3])]
    copies += [pltpu.make_async_copy(weight.at[a], weight_out.at[a], sems.at[a]) for a in range(3)]
    for copy in copies:
        copy.start()
    head_rows[...] = jnp.zeros_like(head_rows)
    normed[...] = rms_silu(main[...].astype(F32)).astype(BF16)
    copies[0].wait()
    for a in range(3):
        for b in range(3):
            for c in range(3):
                start = (3 * a + c) * 128 + (2 - b) * depth
                head_rows[start : start + depth] = head_in[a, b, c]
    for copy in copies[1:]:
        copy.wait()


def section_kernel(
    cols, depth, place_in_mesh, main, near, far, conv_win, head_win, weight, head_rows, ready, out, normed, hidden
):
    frames, rows, win, width = main.shape
    count = frames * rows * win
    normed[0:2, 1 : rows + 1] = conv_win[...]
    normed[2:, 1 : rows + 1] = ready[...]
    odd = place_in_mesh[1] % 2 == 1
    for edge, when_odd, when_even in ((0, near, far), (rows + 1, far, near)):
        cached = jnp.where(odd, when_odd[0:2], when_even[0:2])
        values = jnp.where(odd, when_odd[2:].astype(F32), when_even[2:].astype(F32))
        normed[0:2, edge] = cached
        normed[2:, edge] = rms_silu(values).astype(BF16)
    before = 2 * rows * win
    hidden[0:before] = head_win[...].reshape(before, width)

    together = 4
    chunk = together * rows * win
    place = iota((chunk, 1), 0) % win
    inside = (place < STEP) & (STEP * place_in_mesh[0] + place < cols)
    for first in range(0, frames, together):
        left = jnp.concatenate(
            [
                normed[first + a : first + a + together, b : b + rows].reshape(chunk, width)
                for a in range(3)
                for b in range(3)
            ],
            axis=1,
        )
        right = jnp.concatenate(
            [weight[:, :, c].reshape(9 * width, width) for c in range(3)], axis=1
        )
        sums = jnp.dot(left, right, preferred_element_type=F32)
        update = (
            sums[:, :width]
            + pltpu.roll(sums[:, width : 2 * width], chunk - 1, 0)
            + pltpu.roll(sums[:, 2 * width :], chunk - 2, 0)
        )
        own = main[first : first + together].astype(F32).reshape(chunk, width)
        residual = (pltpu.roll(own, chunk - 1, 0) + update).astype(BF16).astype(F32)
        start = before + first * rows * win
        hidden[start : start + chunk] = jnp.where(inside, rms_silu(residual), 0.0).astype(BF16)

    taps = rows_times_rows(hidden[...], head_rows[...])
    shifted = []
    for c in range(3):
        total = jnp.zeros((count, 128), F32)
        for a in range(3):
            total += taps[
                a * rows * win : a * rows * win + count, (3 * a + c) * 128 : (3 * a + c + 1) * 128
            ]
        shifted.append(total if c == 2 else pltpu.roll(total, 2 - c, 0))
    total = (shifted[0] + shifted[1] + shifted[2]).reshape(frames, rows, win, 128)
    for frame in range(frames):
        piece = total[frame, 0]
        for row in range(1, rows):
            piece += pltpu.roll(total[frame, row], depth * row, 1)
        piece = piece.astype(BF16)
        for target in range(out.shape[1]):
            out[frame, target] = piece


def folded_kernel(patch, qkv, folded, gram, parts, qkv_in, sems):
    depth = patch.shape[2]
    width = patch.shape[3]
    positions = 4 * depth
    chunks = sems.shape[0]
    share = qkv.shape[0] // chunks
    copies = []
    for index in range(chunks):
        part = pl.ds(index * share, share)
        copies.append(pltpu.make_async_copy(qkv.at[part], qkv_in.at[part], sems.at[index]))
        copies[-1].start()

    def stacked(values):
        pieces = list(three_parts(values))
        pieces.append(jnp.zeros_like(pieces[0]))
        return jnp.concatenate(pieces, axis=1)

    for b in range(2):
        for a in range(2):
            weights = patch[a, b].astype(F32)
            centred = weights - jnp.mean(weights, axis=1, keepdims=True)
            for index, part in enumerate(three_parts(centred)):
                start = index * positions + (2 * b + a) * depth
                parts[start : start + depth] = part
    product = rows_times_rows(parts[...], parts[...])
    total = jnp.zeros((positions, positions), F32)
    for i in range(3):
        for k in range(3):
            total += product[
                i * positions : (i + 1) * positions, k * positions : (k + 1) * positions
            ]
    gram[...] = stacked(total / width)

    for index in range(chunks):
        copies[index].wait()
        part = pl.ds(index * share, share)
        product = rows_times_rows(qkv_in[part], parts[...])
        folded[part] = stacked(
            product[:, :positions]
            + product[:, positions : 2 * positions]
            + product[:, 2 * positions :]
        )


def project_kernel(depth, pieces, folded, gram, out, sums, patches, columns, staged, sems):
    groups, blocks, win, lanes = pieces.shape
    positions = 4 * depth
    tokens = patches.shape[0]
    half = tokens // (2 * blocks)
    pad = (half + 7) // 8 * 8

    shape = (2 * pad, groups * win)
    row = iota(shape, 0)
    place = iota(shape, 1)
    odd = (row >= pad).astype(jnp.int32)
    patch_col = row - pad * odd
    column = STEP * (place // win) + place % win - 1
    pick = ((column == 2 * patch_col + odd) & (patch_col < half)).astype(BF16)
    for block in range(blocks):
        source = pieces[:, block].reshape(groups * win, lanes)
        sums[block] = jnp.dot(pick, source, preferred_element_type=F32)
    slot = iota((1, lanes), 1) // depth
    turned = [None] * blocks
    for block in range(blocks):
        for near in (block, block + 1):
            if near < blocks and turned[near] is None:
                turned[near] = pltpu.roll(sums[near], 4 * depth, 1)
        total = sums[block]
        if block > 0:
            total += jnp.where(slot == 1, turned[block - 1], 0.0)
        if block < blocks - 1:
            total += jnp.where(slot == 4, turned[block + 1], 0.0)
        for i in range(2):
            start = (1 + 2 * i) * depth
            even = pltpu.roll(total[0:pad], lanes - start, 1)
            uneven = pltpu.roll(total[pad:], (lanes + 2 * depth - start) % lanes, 1)
            patch = jnp.where(slot < 2, even, jnp.where(slot < 4, uneven, 0.0))
            first = (2 * block + i) * half
            patches[first : first + half] = patch[0:half]
    turned = jnp.transpose(patches[...])[0:positions]
    rounded = turned.astype(BF16)
    for index in range(4):
        columns[index * positions : (index + 1) * positions] = rounded
    product = jnp.dot(gram[...], columns[...], preferred_element_type=F32)
    variance = jnp.sum(product * rounded.astype(F32), axis=0, keepdims=True)
    scale = lax.rsqrt(jnp.maximum(variance, 0.0) + EPS)
    chunks = sems.shape[0]
    share = folded.shape[0] // chunks
    copies = []
    for index in range(chunks):
        part = pl.ds(index * share, share)
        product = jnp.dot(folded[part], columns[...], preferred_element_type=F32)
        staged[part] = (product * scale).astype(BF16)
        copies.append(pltpu.make_async_copy(staged.at[part], out.at[part], sems.at[index]))
        copies[-1].start()
    for copy in copies:
        copy.wait()


ON_CHIP = pl.BlockSpec(memory_space=pltpu.VMEM)
IN_HBM = pl.BlockSpec(memory_space=pltpu.HBM)
SCALAR = pl.BlockSpec(memory_space=pltpu.SMEM)


def params(mebibytes):
    return pltpu.CompilerParams(vmem_limit_bytes=mebibytes << 20)


def in_hbm(array):
    return pltpu.with_memory_space_constraint(array, pltpu.HBM)


def feature_windows(features, groups):
    rows, cols, width = features.shape
    return pl.pallas_call(
        functools.partial(feature_windows_kernel, groups),
        in_specs=[IN_HBM],
        out_specs=IN_HBM,
        out_shape=pltpu.HBM((groups, rows, WIN, width), BF16),
        scratch_shapes=[
            pltpu.VMEM(features.shape, BF16),
            pltpu.VMEM((groups, rows, WIN, width), BF16),
            pltpu.SemaphoreType.DMA((rows,)),
            pltpu.SemaphoreType.DMA((rows,)),
        ],
        compiler_params=params(8),
        name="feature_windows",
    )(in_hbm(features))


def cache_windows(position, conv_cache, head_cache):
    frames, rows, cols, width = conv_cache.shape
    window = pltpu.VMEM((frames, rows, WIN, width), BF16)
    return pl.pallas_call(
        cache_windows_kernel,
        in_specs=[SCALAR, IN_HBM, IN_HBM],
        out_specs=[ON_CHIP] * 2,
        out_shape=[window, window],
        scratch_shapes=[
            pltpu.VMEM(conv_cache.shape, BF16),
            pltpu.VMEM(head_cache.shape, BF16),
            pltpu.SemaphoreType.DMA((2,)),
        ],
        compiler_params=params(8),
        name="cache_windows",
    )(position, in_hbm(conv_cache), in_hbm(head_cache))


def weights_on_chip(main, weight, head):
    return pl.pallas_call(
        weights_kernel,
        in_specs=[ON_CHIP, IN_HBM, IN_HBM],
        out_specs=[ON_CHIP] * 3,
        out_shape=[
            pltpu.VMEM(weight.shape, BF16),
            pltpu.VMEM((9 * 128, weight.shape[3]), BF16),
            pltpu.VMEM(main.shape, BF16),
        ],
        scratch_shapes=[pltpu.VMEM(head.shape, BF16), pltpu.SemaphoreType.DMA((4,))],
        compiler_params=params(8),
        name="weights_on_chip",
    )(main, in_hbm(weight), in_hbm(head))


def section(place_in_mesh, main, near, far, conv_win, head_win, weight, head_rows, ready, cols, depth, blocks):
    frames, rows, win, width = main.shape
    return pl.pallas_call(
        functools.partial(section_kernel, cols, depth),
        in_specs=[SCALAR] + [ON_CHIP] * 8,
        out_specs=ON_CHIP,
        out_shape=pltpu.VMEM((frames, blocks, win, 128), BF16),
        scratch_shapes=[
            pltpu.VMEM((frames + 2, rows + 2, win, width), BF16),
            pltpu.VMEM(((frames + 2) * rows * win, width), BF16),
        ],
        compiler_params=params(20),
        name="section",
    )(place_in_mesh, main, near, far, conv_win, head_win, weight, head_rows, ready)


def folded_weights(patch, qkv):
    positions = 4 * patch.shape[2]
    chunks = 4
    return pl.pallas_call(
        folded_kernel,
        in_specs=[ON_CHIP, IN_HBM],
        out_specs=[ON_CHIP] * 2,
        out_shape=[
            pltpu.VMEM((qkv.shape[0], 4 * positions), BF16),
            pltpu.VMEM((positions, 4 * positions), BF16),
        ],
        scratch_shapes=[
            pltpu.VMEM((3 * positions, patch.shape[3]), BF16),
            pltpu.VMEM(qkv.shape, BF16),
            pltpu.SemaphoreType.DMA((chunks,)),
        ],
        compiler_params=params(24),
        name="folded_weights",
    )(patch, in_hbm(qkv))


def project(pieces, folded, gram, cols, depth):
    groups, blocks, win, lanes = pieces.shape
    half = cols // 2
    pad = (half + 7) // 8 * 8
    tokens = 2 * blocks * half
    outputs = folded.shape[0]
    chunks = 4
    return pl.pallas_call(
        functools.partial(project_kernel, depth),
        in_specs=[ON_CHIP] * 3,
        out_specs=IN_HBM,
        out_shape=pltpu.HBM((outputs, tokens), BF16),
        scratch_shapes=[
            pltpu.VMEM((blocks, 2 * pad, lanes), F32),
            pltpu.VMEM((tokens, lanes), F32),
            pltpu.VMEM((16 * depth, tokens), BF16),
            pltpu.VMEM((outputs, tokens), BF16),
            pltpu.SemaphoreType.DMA((chunks,)),
        ],
        compiler_params=params(20),
        name="project",
    )(pieces, folded, gram)


def swaps(count, first):
    pairs = [(i, i + 1) for i in range(first, count - 1, 2)]
    return pairs + [(target, source) for source, target in pairs]


def local(features, conv_cache, head_cache, conv_weight, head_weight, patch_weight, qkv_weight):
    groups = lax.axis_size("tm")
    blocks = lax.axis_size("rows")
    _, rows, cols, width = features.shape
    depth = head_weight.shape[-1]
    local_cols = qkv_weight.shape[2]
    block = lax.axis_index("rows")
    place_in_mesh = jnp.stack([lax.axis_index("tm"), block]).astype(jnp.int32)
    head = head_weight.transpose(0, 1, 2, 4, 3)
    flat_qkv = qkv_weight.transpose(1, 2, 0).reshape(3 * local_cols, qkv_weight.shape[0])

    main = lax.all_to_all(feature_windows(features[0], groups), "tm", 0, 0, tiled=True)
    conv_win, head_win = cache_windows(place_in_mesh, conv_cache, head_cache)
    def edge(row):
        return jnp.concatenate(
            [lax.dynamic_index_in_dim(part, row, 1, False) for part in (conv_win, main)]
        )

    odd = block % 2
    far = lax.ppermute(edge((rows - 1) * odd), "rows", swaps(blocks, 1))
    near = lax.ppermute(edge((rows - 1) * (1 - odd)), "rows", swaps(blocks, 0))
    weight, head_rows, ready = weights_on_chip(main, conv_weight, head)
    partial = section(
        place_in_mesh, main, near, far, conv_win, head_win, weight, head_rows, ready, cols, depth, blocks
    )
    pieces = lax.all_to_all(
        partial.reshape(groups * blocks, WIN, 128), ("tm", "rows"), 0, 0, tiled=True
    ).reshape(groups, blocks, WIN, 128)
    folded, gram = folded_weights(patch_weight, flat_qkv)
    result = project(pieces, folded, gram, cols, depth)
    return result.reshape(3, local_cols, result.shape[1]).transpose(2, 0, 1)


def solution(mesh):
    return jax.shard_map(
        local,
        mesh=mesh,
        in_specs=(
            P("tm", "rows", None, None),
            P(None, "rows", None, None),
            P(None, "rows", None, None),
            P(),
            P(),
            P(),
            P(None, None, "rows"),
        ),
        out_specs=P("tm", None, "rows"),
        check_vma=False,
    )
```

```python
import functools

import jax
import jax.numpy as jnp
from jax import lax
from jax.experimental import pallas as pl
from jax.experimental.pallas import tpu as pltpu
from jax.sharding import PartitionSpec as P

F32 = jnp.float32
BF16 = jnp.bfloat16
EPS = 1e-06
STEP = 14
EARLY = 2
WIN = 16


def iota(shape, axis):
    return lax.broadcasted_iota(jnp.int32, shape, axis)


def rms_silu(values):
    scaled = values * lax.rsqrt(jnp.mean(values * values, axis=-1, keepdims=True) + EPS)
    return scaled / (1.0 + jnp.exp(-scaled))


def three_parts(values):
    first = values.astype(BF16)
    rest = values - first.astype(F32)
    second = rest.astype(BF16)
    third = (rest - second.astype(F32)).astype(BF16)
    return first, second, third


def rows_times_rows(left, right):
    return lax.dot_general(left, right, (((1,), (1,)), ((), ())), preferred_element_type=F32)


def feature_windows_kernel(groups, features, send, rows_in, windows, sems_in, sems_out):
    rows, cols, width = features.shape
    copies = [
        pltpu.make_async_copy(features.at[row], rows_in.at[row], sems_in.at[row])
        for row in range(rows)
    ]
    for copy in copies:
        copy.start()
    after = STEP * (groups - 1) + WIN - 1 - cols
    results = []
    for row in range(rows):
        copies[row].wait()
        values = jnp.concatenate(
            [
                jnp.zeros((8, width), F32),
                rows_in[row].astype(F32),
                jnp.zeros(((after + 7) // 8 * 8, width), F32),
            ],
            axis=0,
        )
        for group in range(groups):
            first = 8 + STEP * group - 1
            windows[group, row] = values[first : first + WIN].astype(BF16)
        part = pl.ds(row, 1)
        results.append(
            pltpu.make_async_copy(windows.at[:, part], send.at[:, part], sems_out.at[row])
        )
        results[-1].start()
    for copy in results:
        copy.wait()


def cache_windows_kernel(
    position, conv_cache, head_cache, weight, conv_win, head_win, early, conv_in, head_in, sems
):
    frames, rows, cols, _ = conv_cache.shape
    copies = [
        pltpu.make_async_copy(conv_cache, conv_in, sems.at[0]),
        pltpu.make_async_copy(head_cache, head_in, sems.at[1]),
        pltpu.make_async_copy(weight.at[pl.ds(0, early.shape[0])], early, sems.at[2]),
    ]
    for copy in copies:
        copy.start()
    shape = (WIN, cols)
    place = iota(shape, 0)
    first = STEP * position[0]
    pick_conv = (iota(shape, 1) == first + place - 1).astype(BF16)
    pick_head = ((iota(shape, 1) == first + place) & (place < STEP)).astype(BF16)
    for copy, pick, source, out in (
        (copies[0], pick_conv, conv_in, conv_win),
        (copies[1], pick_head, head_in, head_win),
    ):
        copy.wait()
        for frame in range(frames):
            for row in range(rows):
                out[frame, row] = jnp.dot(
                    pick, source[frame, row], preferred_element_type=F32
                ).astype(BF16)
    copies[2].wait()


def after_block(sums, features, place_in_mesh, cols):
    count, width = features.shape
    update = (
        sums[:, :width]
        + pltpu.roll(sums[:, width : 2 * width], count - 1, 0)
        + pltpu.roll(sums[:, 2 * width :], count - 2, 0)
    )
    residual = (pltpu.roll(features, count - 1, 0) + update).astype(BF16).astype(F32)
    place = iota((count, 1), 0) % WIN
    inside = (place < STEP) & (STEP * place_in_mesh[0] + place < cols)
    return jnp.where(inside, rms_silu(residual), 0.0).astype(BF16)


def column_taps(weights):
    return jnp.concatenate(
        [jnp.concatenate([weight[c] for c in range(weight.shape[0])], axis=1) for weight in weights],
        axis=0,
    )


def inner_kernel(
    cols, place_in_mesh, main, conv_win, early, weight, head, late, head_rows, normed, inner, head_in, sems
):
    frames, rows, win, width = main.shape
    depth = head.shape[3]
    head_copy = pltpu.make_async_copy(head, head_in, sems.at[late.shape[0]])
    copies = [
        pltpu.make_async_copy(weight.at[EARLY + i], late.at[i], sems.at[i])
        for i in range(late.shape[0])
    ]
    head_copy.start()
    for copy in copies:
        copy.start()
    normed[0:2] = conv_win[...]
    normed[2:] = rms_silu(main[...].astype(F32)).astype(BF16)
    head_rows[...] = jnp.zeros_like(head_rows)
    head_copy.wait()
    for a in range(3):
        for b in range(3):
            for c in range(3):
                slot = 2 * a + c if c < 2 else 6 + a
                start = slot * 64 + (2 - b) * depth
                head_rows[start : start + depth] = head_in[a, b, c]
    count = frames * (rows - 2) * win
    sums = None
    for pairs in (range(0, EARLY), range(EARLY, 5), range(5, 8), range(8, 9)):
        left = jnp.concatenate(
            [
                normed[pair // 3 : pair // 3 + frames, pair % 3 : pair % 3 + rows - 2].reshape(
                    count, width
                )
                for pair in pairs
            ],
            axis=1,
        )
        weights = []
        for pair in pairs:
            if pair < EARLY:
                weights.append(early[pair])
            else:
                copies[pair - EARLY].wait()
                weights.append(late[pair - EARLY])
        product = jnp.dot(left, column_taps(weights), preferred_element_type=F32)
        sums = product if sums is None else sums + product
    own = main[:, 1 : rows - 1].astype(F32).reshape(count, width)
    inner[...] = after_block(sums, own, place_in_mesh, cols).reshape(inner.shape)


def section_kernel(
    cols, depth, place_in_mesh, main, near, far, head_win, early, late, head_rows, normed, inner, out, edges, hidden, pieces, sems
):
    frames, rows, win, width = main.shape
    count = frames * rows * win
    odd = place_in_mesh[1] % 2 == 1
    for edge, when_odd, when_even in ((0, near, far), (1, far, near)):
        edges[edge, 0:2] = jnp.where(odd, when_odd[0:2], when_even[0:2])
        values = jnp.where(odd, when_odd[2:].astype(F32), when_even[2:].astype(F32))
        edges[edge, 2:] = rms_silu(values).astype(BF16)
    hidden[0:2] = head_win[...]
    hidden[2:, 1 : rows - 1] = inner[...]

    def both(first, second):
        return jnp.concatenate([first[:, None], second[:, None]], axis=1).reshape(-1, width)

    columns = []
    for a in range(3):
        part = slice(a, a + frames)
        columns.append(both(edges[0, part], normed[part, rows - 2]))
        columns.append(both(normed[part, 0], normed[part, rows - 1]))
        columns.append(both(normed[part, 1], edges[1, part]))
    left = jnp.concatenate(columns, axis=1)
    weights = [early[i] for i in range(EARLY)] + [late[i] for i in range(late.shape[0])]
    sums = jnp.dot(left, column_taps(weights), preferred_element_type=F32)
    own = both(main[:, 0].astype(F32), main[:, rows - 1].astype(F32))
    outer = after_block(sums, own, place_in_mesh, cols).reshape(frames, 2, win, width)
    hidden[2:, 0] = outer[:, 0]
    hidden[2:, rows - 1] = outer[:, 1]

    before = rows * win
    taps = rows_times_rows(hidden[...].reshape(count + 2 * before, width), head_rows[...])
    pair = sum(taps[a * before : a * before + count, a * 128 : (a + 1) * 128] for a in range(3))
    last = taps[0:count, 384:512] + pltpu.roll(taps[before : before + count, 384:512], 64, 1)
    last += taps[2 * before : 2 * before + count, 512:576 + 64]
    total = pltpu.roll(pair, 2, 0) + pltpu.roll(pltpu.roll(pair, 64, 1), 1, 0) + last
    total = jnp.where(iota((1, 128), 1) < 64, total, 0.0).reshape(frames, rows, win, 128)
    copies = []
    for frame in range(frames):
        piece = total[frame, 0]
        for row in range(1, rows):
            piece += pltpu.roll(total[frame, row], depth * row, 1)
        piece = piece.astype(BF16)
        for target in range(out.shape[1]):
            pieces[frame, target] = piece
        copies.append(pltpu.make_async_copy(pieces.at[frame], out.at[frame], sems.at[frame]))
        copies[-1].start()
    for copy in copies:
        copy.wait()


def folded_kernel(patch, qkv, folded, gram, parts, qkv_in, sems):
    depth = patch.shape[2]
    width = patch.shape[3]
    positions = 4 * depth
    chunks = sems.shape[0]
    share = qkv.shape[0] // chunks
    copies = []
    for index in range(chunks):
        part = pl.ds(index * share, share)
        copies.append(pltpu.make_async_copy(qkv.at[part], qkv_in.at[part], sems.at[index]))
        copies[-1].start()

    def stacked(values):
        pieces = list(three_parts(values))
        pieces.append(jnp.zeros_like(pieces[0]))
        return jnp.concatenate(pieces, axis=1)

    for b in range(2):
        for a in range(2):
            weights = patch[a, b].astype(F32)
            centred = weights - jnp.mean(weights, axis=1, keepdims=True)
            for index, part in enumerate(three_parts(centred)):
                start = index * positions + (2 * b + a) * depth
                parts[start : start + depth] = part
    product = rows_times_rows(parts[...], parts[...])
    total = jnp.zeros((positions, positions), F32)
    for i in range(3):
        for k in range(3):
            total += product[
                i * positions : (i + 1) * positions, k * positions : (k + 1) * positions
            ]
    gram[...] = stacked(total / width)

    for index in range(chunks):
        copies[index].wait()
        part = pl.ds(index * share, share)
        product = rows_times_rows(qkv_in[part], parts[...])
        folded[part] = stacked(
            product[:, :positions]
            + product[:, positions : 2 * positions]
            + product[:, 2 * positions :]
        )


def project_kernel(depth, pieces, folded, gram, out, sums, patches, columns, staged, sems):
    groups, blocks, win, lanes = pieces.shape
    positions = 4 * depth
    tokens = patches.shape[0]
    half = tokens // (2 * blocks)
    pad = (half + 7) // 8 * 8

    shape = (2 * pad, groups * win)
    row = iota(shape, 0)
    place = iota(shape, 1)
    odd = (row >= pad).astype(jnp.int32)
    patch_col = row - pad * odd
    column = STEP * (place // win) + place % win - 1
    pick = ((column == 2 * patch_col + odd) & (patch_col < half)).astype(BF16)
    for block in range(blocks):
        source = pieces[:, block].reshape(groups * win, lanes)
        sums[block] = jnp.dot(pick, source, preferred_element_type=F32)
    slot = iota((1, lanes), 1) // depth
    turned = [None] * blocks
    for block in range(blocks):
        for near in (block, block + 1):
            if near < blocks and turned[near] is None:
                turned[near] = pltpu.roll(sums[near], 4 * depth, 1)
        total = sums[block]
        if block > 0:
            total += jnp.where(slot == 1, turned[block - 1], 0.0)
        if block < blocks - 1:
            total += jnp.where(slot == 4, turned[block + 1], 0.0)
        for i in range(2):
            start = (1 + 2 * i) * depth
            even = pltpu.roll(total[0:pad], lanes - start, 1)
            uneven = pltpu.roll(total[pad:], (lanes + 2 * depth - start) % lanes, 1)
            patch = jnp.where(slot < 2, even, jnp.where(slot < 4, uneven, 0.0))
            first = (2 * block + i) * half
            patches[first : first + half] = patch[0:half]
    turned = jnp.transpose(patches[...])[0:positions]
    rounded = turned.astype(BF16)
    for index in range(4):
        columns[index * positions : (index + 1) * positions] = rounded
    product = jnp.dot(gram[...], columns[...], preferred_element_type=F32)
    variance = jnp.sum(product * rounded.astype(F32), axis=0, keepdims=True)
    scale = lax.rsqrt(jnp.maximum(variance, 0.0) + EPS)
    chunks = sems.shape[0]
    share = folded.shape[0] // chunks
    copies = []
    for index in range(chunks):
        part = pl.ds(index * share, share)
        product = jnp.dot(folded[part], columns[...], preferred_element_type=F32)
        staged[part] = (product * scale).astype(BF16)
        copies.append(pltpu.make_async_copy(staged.at[part], out.at[part], sems.at[index]))
        copies[-1].start()
    for copy in copies:
        copy.wait()


ON_CHIP = pl.BlockSpec(memory_space=pltpu.VMEM)
IN_HBM = pl.BlockSpec(memory_space=pltpu.HBM)
SCALAR = pl.BlockSpec(memory_space=pltpu.SMEM)


def params(mebibytes):
    return pltpu.CompilerParams(vmem_limit_bytes=mebibytes << 20)


def in_hbm(array):
    return pltpu.with_memory_space_constraint(array, pltpu.HBM)


def feature_windows(features, groups):
    rows, cols, width = features.shape
    return pl.pallas_call(
        functools.partial(feature_windows_kernel, groups),
        in_specs=[IN_HBM],
        out_specs=IN_HBM,
        out_shape=pltpu.HBM((groups, rows, WIN, width), BF16),
        scratch_shapes=[
            pltpu.VMEM(features.shape, BF16),
            pltpu.VMEM((groups, rows, WIN, width), BF16),
            pltpu.SemaphoreType.DMA((rows,)),
            pltpu.SemaphoreType.DMA((rows,)),
        ],
        compiler_params=params(8),
        name="feature_windows",
    )(in_hbm(features))


def cache_windows(position, conv_cache, head_cache, weight):
    frames, rows, cols, width = conv_cache.shape
    window = pltpu.VMEM((frames, rows, WIN, width), BF16)
    return pl.pallas_call(
        cache_windows_kernel,
        in_specs=[SCALAR, IN_HBM, IN_HBM, IN_HBM],
        out_specs=[ON_CHIP] * 3,
        out_shape=[window, window, pltpu.VMEM((EARLY,) + weight.shape[1:], BF16)],
        scratch_shapes=[
            pltpu.VMEM(conv_cache.shape, BF16),
            pltpu.VMEM(head_cache.shape, BF16),
            pltpu.SemaphoreType.DMA((3,)),
        ],
        compiler_params=params(8),
        name="cache_windows",
    )(position, in_hbm(conv_cache), in_hbm(head_cache), in_hbm(weight))


def inner_rows(place_in_mesh, main, conv_win, early, weight, head, cols):
    frames, rows, win, width = main.shape
    late = (weight.shape[0] - EARLY,) + weight.shape[1:]
    return pl.pallas_call(
        functools.partial(inner_kernel, cols),
        in_specs=[SCALAR] + [ON_CHIP] * 3 + [IN_HBM] * 2,
        out_specs=[ON_CHIP] * 4,
        out_shape=[
            pltpu.VMEM(late, BF16),
            pltpu.VMEM((10 * 64, width), BF16),
            pltpu.VMEM((frames + 2, rows, win, width), BF16),
            pltpu.VMEM((frames, rows - 2, win, width), BF16),
        ],
        scratch_shapes=[pltpu.VMEM(head.shape, BF16), pltpu.SemaphoreType.DMA((late[0] + 1,))],
        compiler_params=params(20),
        name="inner_rows",
    )(place_in_mesh, main, conv_win, early, in_hbm(weight), in_hbm(head))


def section(place_in_mesh, main, near, far, head_win, early, prepared, cols, depth, blocks):
    frames, rows, win, width = main.shape
    return pl.pallas_call(
        functools.partial(section_kernel, cols, depth),
        in_specs=[SCALAR] + [ON_CHIP] * 9,
        out_specs=IN_HBM,
        out_shape=pltpu.HBM((frames, blocks, win, 128), BF16),
        scratch_shapes=[
            pltpu.VMEM((2, frames + 2, win, width), BF16),
            pltpu.VMEM((frames + 2, rows, win, width), BF16),
            pltpu.VMEM((frames, blocks, win, 128), BF16),
            pltpu.SemaphoreType.DMA((frames,)),
        ],
        compiler_params=params(20),
        name="section",
    )(place_in_mesh, main, near, far, head_win, early, *prepared)


def folded_weights(patch, qkv):
    positions = 4 * patch.shape[2]
    chunks = 4
    return pl.pallas_call(
        folded_kernel,
        in_specs=[ON_CHIP, IN_HBM],
        out_specs=[ON_CHIP] * 2,
        out_shape=[
            pltpu.VMEM((qkv.shape[0], 4 * positions), BF16),
            pltpu.VMEM((positions, 4 * positions), BF16),
        ],
        scratch_shapes=[
            pltpu.VMEM((3 * positions, patch.shape[3]), BF16),
            pltpu.VMEM(qkv.shape, BF16),
            pltpu.SemaphoreType.DMA((chunks,)),
        ],
        compiler_params=params(24),
        name="folded_weights",
    )(patch, in_hbm(qkv))


def project(pieces, folded, gram, cols, depth):
    groups, blocks, win, lanes = pieces.shape
    half = cols // 2
    pad = (half + 7) // 8 * 8
    tokens = 2 * blocks * half
    outputs = folded.shape[0]
    chunks = 4
    return pl.pallas_call(
        functools.partial(project_kernel, depth),
        in_specs=[ON_CHIP] * 3,
        out_specs=IN_HBM,
        out_shape=pltpu.HBM((outputs, tokens), BF16),
        scratch_shapes=[
            pltpu.VMEM((blocks, 2 * pad, lanes), F32),
            pltpu.VMEM((tokens, lanes), F32),
            pltpu.VMEM((16 * depth, tokens), BF16),
            pltpu.VMEM((outputs, tokens), BF16),
            pltpu.SemaphoreType.DMA((chunks,)),
        ],
        compiler_params=params(20),
        name="project",
    )(pieces, folded, gram)


def swaps(count, first):
    pairs = [(i, i + 1) for i in range(first, count - 1, 2)]
    return pairs + [(target, source) for source, target in pairs]


def local(features, conv_cache, head_cache, conv_weight, head_weight, patch_weight, qkv_weight):
    groups = lax.axis_size("tm")
    blocks = lax.axis_size("rows")
    _, rows, cols, width = features.shape
    depth = head_weight.shape[-1]
    local_cols = qkv_weight.shape[2]
    block = lax.axis_index("rows")
    place_in_mesh = jnp.stack([lax.axis_index("tm"), block]).astype(jnp.int32)
    head = head_weight.transpose(0, 1, 2, 4, 3)
    flat_qkv = qkv_weight.transpose(1, 2, 0).reshape(3 * local_cols, qkv_weight.shape[0])

    main = lax.all_to_all(feature_windows(features[0], groups), "tm", 0, 0, tiled=True)
    pairs = conv_weight.reshape((9,) + conv_weight.shape[2:])
    conv_win, head_win, early = cache_windows(place_in_mesh, conv_cache, head_cache, pairs)
    def edge(row):
        return jnp.concatenate(
            [lax.dynamic_index_in_dim(part, row, 1, False) for part in (conv_win, main)]
        )

    odd = block % 2
    far = lax.ppermute(edge((rows - 1) * odd), "rows", swaps(blocks, 1))
    near = lax.ppermute(edge((rows - 1) * (1 - odd)), "rows", swaps(blocks, 0))
    prepared = inner_rows(place_in_mesh, main, conv_win, early, pairs, head, cols)
    partial = section(
        place_in_mesh, main, near, far, head_win, early, prepared, cols, depth, blocks
    )
    pieces = lax.all_to_all(
        partial.reshape(groups * blocks, WIN, 128), ("tm", "rows"), 0, 0, tiled=True
    ).reshape(groups, blocks, WIN, 128)
    folded, gram = folded_weights(patch_weight, flat_qkv)
    result = project(pieces, folded, gram, cols, depth)
    return result.reshape(3, local_cols, result.shape[1]).transpose(2, 0, 1)


def solution(mesh):
    return jax.shard_map(
        local,
        mesh=mesh,
        in_specs=(
            P("tm", "rows", None, None),
            P(None, "rows", None, None),
            P(None, "rows", None, None),
            P(),
            P(),
            P(),
            P(None, None, "rows"),
        ),
        out_specs=P("tm", None, "rows"),
        check_vma=False,
    )
```

```python
import functools

import jax
import jax.numpy as jnp
from jax import lax
from jax.experimental import pallas as pl
from jax.experimental.pallas import tpu as pltpu
from jax.sharding import PartitionSpec as P

F32 = jnp.float32
BF16 = jnp.bfloat16
EPS = 1e-06
STEP = 14
EARLY = 1
WIN = 16


def iota(shape, axis):
    return lax.broadcasted_iota(jnp.int32, shape, axis)


def rms_silu(values):
    scaled = values * lax.rsqrt(jnp.mean(values * values, axis=-1, keepdims=True) + EPS)
    return scaled / (1.0 + jnp.exp(-scaled))


def three_parts(values):
    first = values.astype(BF16)
    rest = values - first.astype(F32)
    second = rest.astype(BF16)
    third = (rest - second.astype(F32)).astype(BF16)
    return first, second, third


def rows_times_rows(left, right):
    return lax.dot_general(left, right, (((1,), (1,)), ((), ())), preferred_element_type=F32)


def feature_windows_kernel(groups, features, send, rows_in, windows, sems_in, sems_out):
    rows, cols, width = features.shape
    copies = [
        pltpu.make_async_copy(features.at[row], rows_in.at[row], sems_in.at[row])
        for row in range(rows)
    ]
    for copy in copies:
        copy.start()
    after = STEP * (groups - 1) + WIN - 1 - cols
    results = []
    for row in range(rows):
        copies[row].wait()
        values = jnp.concatenate(
            [
                jnp.zeros((8, width), F32),
                rows_in[row].astype(F32),
                jnp.zeros(((after + 7) // 8 * 8, width), F32),
            ],
            axis=0,
        )
        for group in range(groups):
            first = 8 + STEP * group - 1
            windows[group, row] = values[first : first + WIN].astype(BF16)
        part = pl.ds(row, 1)
        results.append(
            pltpu.make_async_copy(windows.at[:, part], send.at[:, part], sems_out.at[row])
        )
        results[-1].start()
    for copy in results:
        copy.wait()


def cache_windows_kernel(
    position, conv_cache, head_cache, weight, conv_win, head_win, early, conv_in, head_in, sems
):
    frames, rows, cols, _ = conv_cache.shape
    copies = [
        pltpu.make_async_copy(conv_cache, conv_in, sems.at[0]),
        pltpu.make_async_copy(head_cache, head_in, sems.at[1]),
        pltpu.make_async_copy(weight.at[pl.ds(0, early.shape[0])], early, sems.at[2]),
    ]
    for copy in copies:
        copy.start()
    shape = (WIN, cols)
    place = iota(shape, 0)
    first = STEP * position[0]
    pick_conv = (iota(shape, 1) == first + place - 1).astype(BF16)
    pick_head = ((iota(shape, 1) == first + place) & (place < STEP)).astype(BF16)
    for copy, pick, source, out in (
        (copies[0], pick_conv, conv_in, conv_win),
        (copies[1], pick_head, head_in, head_win),
    ):
        copy.wait()
        for frame in range(frames):
            for row in range(rows):
                out[frame, row] = jnp.dot(
                    pick, source[frame, row], preferred_element_type=F32
                ).astype(BF16)
    copies[2].wait()


def after_block(sums, features, place_in_mesh, cols):
    count, width = features.shape
    update = (
        sums[:, :width]
        + pltpu.roll(sums[:, width : 2 * width], count - 1, 0)
        + pltpu.roll(sums[:, 2 * width :], count - 2, 0)
    )
    residual = (pltpu.roll(features, count - 1, 0) + update).astype(BF16).astype(F32)
    place = iota((count, 1), 0) % WIN
    inside = (place < STEP) & (STEP * place_in_mesh[0] + place < cols)
    return jnp.where(inside, rms_silu(residual), 0.0).astype(BF16)


def column_taps(weights):
    return jnp.concatenate(
        [
            jnp.concatenate([weight[b, c] for c in range(weight.shape[1])], axis=1)
            for weight in weights
            for b in range(weight.shape[0])
        ],
        axis=0,
    )


def inner_kernel(
    cols,
    place_in_mesh,
    main,
    conv_win,
    early,
    weight,
    head,
    late,
    head_rows,
    normed,
    inner,
    head_in,
    sums,
    sems,
):
    frames, rows, win, width = main.shape
    depth = head.shape[3]
    taps = late.shape[0]

    def arriving(i):
        return pltpu.make_async_copy(weight.at[EARLY + i], late.at[i], sems.at[i])

    for i in range(taps):
        arriving(i).start()
    head_copy = pltpu.make_async_copy(head, head_in, sems.at[taps])
    head_copy.start()
    normed[0:2] = conv_win[...]
    normed[2:] = rms_silu(main[...].astype(F32)).astype(BF16)
    head_rows[...] = jnp.zeros_like(head_rows)
    count = frames * (rows - 2) * win

    def product(a, weights):
        left = jnp.concatenate(
            [
                normed[pl.ds(a, frames), b : b + rows - 2].reshape(count, width)
                for b in range(3)
            ],
            axis=1,
        )
        return jnp.dot(left, column_taps([weights]), preferred_element_type=F32)

    sums[...] = product(0, early[0])

    def step(i, carry):
        arriving(i).wait()
        sums[...] += product(EARLY + i, late[i])
        return carry

    lax.fori_loop(0, taps, step, 0)
    own = main[:, 1 : rows - 1].astype(F32).reshape(count, width)
    inner[...] = after_block(sums[...], own, place_in_mesh, cols).reshape(inner.shape)
    head_copy.wait()
    for a in range(3):
        for b in range(3):
            for c in range(3):
                slot = 2 * a + c if c < 2 else 6 + a
                start = slot * 64 + (2 - b) * depth
                head_rows[start : start + depth] = head_in[a, b, c]


def section_kernel(
    cols, depth, place_in_mesh, main, near, far, head_win, early, late, head_rows, normed, inner, out, edges, hidden, pieces, sems
):
    frames, rows, win, width = main.shape
    count = frames * rows * win
    odd = place_in_mesh[1] % 2 == 1
    for edge, when_odd, when_even in ((0, near, far), (1, far, near)):
        edges[edge, 0:2] = jnp.where(odd, when_odd[0:2], when_even[0:2])
        values = jnp.where(odd, when_odd[2:].astype(F32), when_even[2:].astype(F32))
        edges[edge, 2:] = rms_silu(values).astype(BF16)
    hidden[0:2] = head_win[...]
    hidden[2:, 1 : rows - 1] = inner[...]

    def both(first, second):
        return jnp.concatenate([first[:, None], second[:, None]], axis=1).reshape(-1, width)

    columns = []
    for a in range(3):
        part = slice(a, a + frames)
        columns.append(both(edges[0, part], normed[part, rows - 2]))
        columns.append(both(normed[part, 0], normed[part, rows - 1]))
        columns.append(both(normed[part, 1], edges[1, part]))
    left = jnp.concatenate(columns, axis=1)
    weights = [early[i] for i in range(EARLY)] + [late[i] for i in range(late.shape[0])]
    sums = jnp.dot(left, column_taps(weights), preferred_element_type=F32)
    own = both(main[:, 0].astype(F32), main[:, rows - 1].astype(F32))
    outer = after_block(sums, own, place_in_mesh, cols).reshape(frames, 2, win, width)
    hidden[2:, 0] = outer[:, 0]
    hidden[2:, rows - 1] = outer[:, 1]

    before = rows * win
    taps = rows_times_rows(hidden[...].reshape(count + 2 * before, width), head_rows[...])
    pair = sum(taps[a * before : a * before + count, a * 128 : (a + 1) * 128] for a in range(3))
    last = taps[0:count, 384:512] + pltpu.roll(taps[before : before + count, 384:512], 64, 1)
    last += taps[2 * before : 2 * before + count, 512:576 + 64]
    total = pltpu.roll(pair, 2, 0) + pltpu.roll(pltpu.roll(pair, 64, 1), 1, 0) + last
    total = jnp.where(iota((1, 128), 1) < 64, total, 0.0).reshape(frames, rows, win, 128)
    copies = []
    for frame in range(frames):
        piece = total[frame, 0]
        for row in range(1, rows):
            piece += pltpu.roll(total[frame, row], depth * row, 1)
        piece = piece.astype(BF16)
        for target in range(out.shape[1]):
            pieces[frame, target] = piece
        copies.append(pltpu.make_async_copy(pieces.at[frame], out.at[frame], sems.at[frame]))
        copies[-1].start()
    for copy in copies:
        copy.wait()


def folded_kernel(patch, qkv, folded, gram, parts, qkv_in, sems):
    depth = patch.shape[2]
    width = patch.shape[3]
    positions = 4 * depth
    chunks = sems.shape[0]
    share = qkv.shape[0] // chunks
    copies = []
    for index in range(chunks):
        part = pl.ds(index * share, share)
        copies.append(pltpu.make_async_copy(qkv.at[part], qkv_in.at[part], sems.at[index]))
        copies[-1].start()

    def stacked(values):
        pieces = list(three_parts(values))
        pieces.append(jnp.zeros_like(pieces[0]))
        return jnp.concatenate(pieces, axis=1)

    for b in range(2):
        for a in range(2):
            weights = patch[a, b].astype(F32)
            centred = weights - jnp.mean(weights, axis=1, keepdims=True)
            for index, part in enumerate(three_parts(centred)):
                start = index * positions + (2 * b + a) * depth
                parts[start : start + depth] = part
    product = rows_times_rows(parts[...], parts[...])
    total = jnp.zeros((positions, positions), F32)
    for i in range(3):
        for k in range(3):
            total += product[
                i * positions : (i + 1) * positions, k * positions : (k + 1) * positions
            ]
    gram[...] = stacked(total / width)

    for index in range(chunks):
        copies[index].wait()
        part = pl.ds(index * share, share)
        product = rows_times_rows(qkv_in[part], parts[...])
        folded[part] = stacked(
            product[:, :positions]
            + product[:, positions : 2 * positions]
            + product[:, 2 * positions :]
        )


def project_kernel(depth, pieces, folded, gram, out, sums, patches, columns, staged, sems):
    groups, blocks, win, lanes = pieces.shape
    positions = 4 * depth
    tokens = patches.shape[0]
    half = tokens // (2 * blocks)
    pad = (half + 7) // 8 * 8

    shape = (2 * pad, groups * win)
    row = iota(shape, 0)
    place = iota(shape, 1)
    odd = (row >= pad).astype(jnp.int32)
    patch_col = row - pad * odd
    column = STEP * (place // win) + place % win - 1
    pick = ((column == 2 * patch_col + odd) & (patch_col < half)).astype(BF16)
    for block in range(blocks):
        source = pieces[:, block].reshape(groups * win, lanes)
        sums[block] = jnp.dot(pick, source, preferred_element_type=F32)
    slot = iota((1, lanes), 1) // depth
    turned = [None] * blocks
    for block in range(blocks):
        for near in (block, block + 1):
            if near < blocks and turned[near] is None:
                turned[near] = pltpu.roll(sums[near], 4 * depth, 1)
        total = sums[block]
        if block > 0:
            total += jnp.where(slot == 1, turned[block - 1], 0.0)
        if block < blocks - 1:
            total += jnp.where(slot == 4, turned[block + 1], 0.0)
        for i in range(2):
            start = (1 + 2 * i) * depth
            even = pltpu.roll(total[0:pad], lanes - start, 1)
            uneven = pltpu.roll(total[pad:], (lanes + 2 * depth - start) % lanes, 1)
            patch = jnp.where(slot < 2, even, jnp.where(slot < 4, uneven, 0.0))
            first = (2 * block + i) * half
            patches[first : first + half] = patch[0:half]
    turned = jnp.transpose(patches[...])[0:positions]
    rounded = turned.astype(BF16)
    for index in range(4):
        columns[index * positions : (index + 1) * positions] = rounded
    product = jnp.dot(gram[...], columns[...], preferred_element_type=F32)
    variance = jnp.sum(product * rounded.astype(F32), axis=0, keepdims=True)
    scale = lax.rsqrt(jnp.maximum(variance, 0.0) + EPS)
    chunks = sems.shape[0]
    share = folded.shape[0] // chunks
    copies = []
    for index in range(chunks):
        part = pl.ds(index * share, share)
        product = jnp.dot(folded[part], columns[...], preferred_element_type=F32)
        staged[part] = (product * scale).astype(BF16)
        copies.append(pltpu.make_async_copy(staged.at[part], out.at[part], sems.at[index]))
        copies[-1].start()
    for copy in copies:
        copy.wait()


ON_CHIP = pl.BlockSpec(memory_space=pltpu.VMEM)
IN_HBM = pl.BlockSpec(memory_space=pltpu.HBM)
SCALAR = pl.BlockSpec(memory_space=pltpu.SMEM)


def params(mebibytes):
    return pltpu.CompilerParams(vmem_limit_bytes=mebibytes << 20)


def in_hbm(array):
    return pltpu.with_memory_space_constraint(array, pltpu.HBM)


def feature_windows(features, groups):
    rows, cols, width = features.shape
    return pl.pallas_call(
        functools.partial(feature_windows_kernel, groups),
        in_specs=[IN_HBM],
        out_specs=IN_HBM,
        out_shape=pltpu.HBM((groups, rows, WIN, width), BF16),
        scratch_shapes=[
            pltpu.VMEM(features.shape, BF16),
            pltpu.VMEM((groups, rows, WIN, width), BF16),
            pltpu.SemaphoreType.DMA((rows,)),
            pltpu.SemaphoreType.DMA((rows,)),
        ],
        compiler_params=params(8),
        name="feature_windows",
    )(in_hbm(features))


def cache_windows(position, conv_cache, head_cache, weight):
    frames, rows, cols, width = conv_cache.shape
    window = pltpu.VMEM((frames, rows, WIN, width), BF16)
    return pl.pallas_call(
        cache_windows_kernel,
        in_specs=[SCALAR, IN_HBM, IN_HBM, IN_HBM],
        out_specs=[ON_CHIP] * 3,
        out_shape=[window, window, pltpu.VMEM((EARLY,) + weight.shape[1:], BF16)],
        scratch_shapes=[
            pltpu.VMEM(conv_cache.shape, BF16),
            pltpu.VMEM(head_cache.shape, BF16),
            pltpu.SemaphoreType.DMA((3,)),
        ],
        compiler_params=params(8),
        name="cache_windows",
    )(position, in_hbm(conv_cache), in_hbm(head_cache), in_hbm(weight))


def inner_rows(place_in_mesh, main, conv_win, early, weight, head, cols):
    frames, rows, win, width = main.shape
    late = (weight.shape[0] - EARLY,) + weight.shape[1:]
    return pl.pallas_call(
        functools.partial(inner_kernel, cols),
        in_specs=[SCALAR] + [ON_CHIP] * 3 + [IN_HBM] * 2,
        out_specs=[ON_CHIP] * 4,
        out_shape=[
            pltpu.VMEM(late, BF16),
            pltpu.VMEM((10 * 64, width), BF16),
            pltpu.VMEM((frames + 2, rows, win, width), BF16),
            pltpu.VMEM((frames, rows - 2, win, width), BF16),
        ],
        scratch_shapes=[
            pltpu.VMEM(head.shape, BF16),
            pltpu.VMEM((frames * (rows - 2) * win, 3 * width), F32),
            pltpu.SemaphoreType.DMA((late[0] + 1,)),
        ],
        compiler_params=params(20),
        name="inner_rows",
    )(place_in_mesh, main, conv_win, early, in_hbm(weight), in_hbm(head))


def section(place_in_mesh, main, near, far, head_win, early, prepared, cols, depth, blocks):
    frames, rows, win, width = main.shape
    return pl.pallas_call(
        functools.partial(section_kernel, cols, depth),
        in_specs=[SCALAR] + [ON_CHIP] * 9,
        out_specs=IN_HBM,
        out_shape=pltpu.HBM((frames, blocks, win, 128), BF16),
        scratch_shapes=[
            pltpu.VMEM((2, frames + 2, win, width), BF16),
            pltpu.VMEM((frames + 2, rows, win, width), BF16),
            pltpu.VMEM((frames, blocks, win, 128), BF16),
            pltpu.SemaphoreType.DMA((frames,)),
        ],
        compiler_params=params(20),
        name="section",
    )(place_in_mesh, main, near, far, head_win, early, *prepared)


def folded_weights(patch, qkv):
    positions = 4 * patch.shape[2]
    chunks = 4
    return pl.pallas_call(
        folded_kernel,
        in_specs=[ON_CHIP, IN_HBM],
        out_specs=[ON_CHIP] * 2,
        out_shape=[
            pltpu.VMEM((qkv.shape[0], 4 * positions), BF16),
            pltpu.VMEM((positions, 4 * positions), BF16),
        ],
        scratch_shapes=[
            pltpu.VMEM((3 * positions, patch.shape[3]), BF16),
            pltpu.VMEM(qkv.shape, BF16),
            pltpu.SemaphoreType.DMA((chunks,)),
        ],
        compiler_params=params(24),
        name="folded_weights",
    )(patch, in_hbm(qkv))


def project(pieces, folded, gram, cols, depth):
    groups, blocks, win, lanes = pieces.shape
    half = cols // 2
    pad = (half + 7) // 8 * 8
    tokens = 2 * blocks * half
    outputs = folded.shape[0]
    chunks = 4
    return pl.pallas_call(
        functools.partial(project_kernel, depth),
        in_specs=[ON_CHIP] * 3,
        out_specs=IN_HBM,
        out_shape=pltpu.HBM((outputs, tokens), BF16),
        scratch_shapes=[
            pltpu.VMEM((blocks, 2 * pad, lanes), F32),
            pltpu.VMEM((tokens, lanes), F32),
            pltpu.VMEM((16 * depth, tokens), BF16),
            pltpu.VMEM((outputs, tokens), BF16),
            pltpu.SemaphoreType.DMA((chunks,)),
        ],
        compiler_params=params(20),
        name="project",
    )(pieces, folded, gram)


def swaps(count, first):
    pairs = [(i, i + 1) for i in range(first, count - 1, 2)]
    return pairs + [(target, source) for source, target in pairs]


def local(features, conv_cache, head_cache, conv_weight, head_weight, patch_weight, qkv_weight):
    groups = lax.axis_size("tm")
    blocks = lax.axis_size("rows")
    _, rows, cols, width = features.shape
    depth = head_weight.shape[-1]
    local_cols = qkv_weight.shape[2]
    block = lax.axis_index("rows")
    place_in_mesh = jnp.stack([lax.axis_index("tm"), block]).astype(jnp.int32)
    head = head_weight.transpose(0, 1, 2, 4, 3)
    flat_qkv = qkv_weight.transpose(1, 2, 0).reshape(3 * local_cols, qkv_weight.shape[0])

    main = lax.all_to_all(feature_windows(features[0], groups), "tm", 0, 0, tiled=True)
    conv_win, head_win, early = cache_windows(place_in_mesh, conv_cache, head_cache, conv_weight)
    def edge(row):
        return jnp.concatenate(
            [lax.dynamic_index_in_dim(part, row, 1, False) for part in (conv_win, main)]
        )

    odd = block % 2
    far = lax.ppermute(edge((rows - 1) * odd), "rows", swaps(blocks, 1))
    near = lax.ppermute(edge((rows - 1) * (1 - odd)), "rows", swaps(blocks, 0))
    prepared = inner_rows(place_in_mesh, main, conv_win, early, conv_weight, head, cols)
    partial = section(
        place_in_mesh, main, near, far, head_win, early, prepared, cols, depth, blocks
    )
    pieces = lax.all_to_all(
        partial.reshape(groups * blocks, WIN, 128), ("tm", "rows"), 0, 0, tiled=True
    ).reshape(groups, blocks, WIN, 128)
    folded, gram = folded_weights(patch_weight, flat_qkv)
    result = project(pieces, folded, gram, cols, depth)
    return result.reshape(3, local_cols, result.shape[1]).transpose(2, 0, 1)


def solution(mesh):
    return jax.shard_map(
        local,
        mesh=mesh,
        in_specs=(
            P("tm", "rows", None, None),
            P(None, "rows", None, None),
            P(None, "rows", None, None),
            P(),
            P(),
            P(),
            P(None, None, "rows"),
        ),
        out_specs=P("tm", None, "rows"),
        check_vma=False,
    )
```

```python
import functools

import jax
import jax.numpy as jnp
from jax import lax
from jax.experimental import pallas as pl
from jax.experimental.pallas import tpu as pltpu
from jax.sharding import PartitionSpec as P

F32 = jnp.float32
BF16 = jnp.bfloat16
EPS = 1e-06
STEP = 14
EARLY = 3
GROUP = 2
WIN = 16


def iota(shape, axis):
    return lax.broadcasted_iota(jnp.int32, shape, axis)


def rms_silu(values):
    scaled = values * lax.rsqrt(jnp.mean(values * values, axis=-1, keepdims=True) + EPS)
    return scaled / (1.0 + jnp.exp(-scaled))


def three_parts(values):
    first = values.astype(BF16)
    rest = values - first.astype(F32)
    second = rest.astype(BF16)
    third = (rest - second.astype(F32)).astype(BF16)
    return first, second, third


def rows_times_rows(left, right):
    return lax.dot_general(left, right, (((1,), (1,)), ((), ())), preferred_element_type=F32)


def feature_windows_kernel(groups, features, send, rows_in, windows, sems_in, sems_out):
    rows, cols, width = features.shape
    copies = [
        pltpu.make_async_copy(features.at[row], rows_in.at[row], sems_in.at[row])
        for row in range(rows)
    ]
    for copy in copies:
        copy.start()
    after = STEP * (groups - 1) + WIN - 1 - cols
    results = []
    for row in range(rows):
        copies[row].wait()
        values = jnp.concatenate(
            [
                jnp.zeros((8, width), F32),
                rows_in[row].astype(F32),
                jnp.zeros(((after + 7) // 8 * 8, width), F32),
            ],
            axis=0,
        )
        for group in range(groups):
            first = 8 + STEP * group - 1
            windows[group, row] = values[first : first + WIN].astype(BF16)
        part = pl.ds(row, 1)
        results.append(
            pltpu.make_async_copy(windows.at[:, part], send.at[:, part], sems_out.at[row])
        )
        results[-1].start()
    for copy in results:
        copy.wait()


def cache_windows_kernel(
    position, conv_cache, head_cache, weight, conv_win, head_win, early, conv_in, head_in, sems
):
    frames, rows, cols, _ = conv_cache.shape
    copies = [
        pltpu.make_async_copy(conv_cache, conv_in, sems.at[0]),
        pltpu.make_async_copy(head_cache, head_in, sems.at[1]),
        pltpu.make_async_copy(weight.at[pl.ds(0, early.shape[0])], early, sems.at[2]),
    ]
    for copy in copies:
        copy.start()
    shape = (WIN, cols)
    place = iota(shape, 0)
    first = STEP * position[0]
    pick_conv = (iota(shape, 1) == first + place - 1).astype(BF16)
    pick_head = ((iota(shape, 1) == first + place) & (place < STEP)).astype(BF16)
    for copy, pick, source, out in (
        (copies[0], pick_conv, conv_in, conv_win),
        (copies[1], pick_head, head_in, head_win),
    ):
        copy.wait()
        for frame in range(frames):
            for row in range(rows):
                out[frame, row] = jnp.dot(
                    pick, source[frame, row], preferred_element_type=F32
                ).astype(BF16)
    copies[2].wait()


def after_block(sums, features, place_in_mesh, cols):
    count, width = features.shape
    update = (
        sums[:, :width]
        + pltpu.roll(sums[:, width : 2 * width], count - 1, 0)
        + pltpu.roll(sums[:, 2 * width :], count - 2, 0)
    )
    residual = (pltpu.roll(features, count - 1, 0) + update).astype(BF16).astype(F32)
    place = iota((count, 1), 0) % WIN
    inside = (place < STEP) & (STEP * place_in_mesh[0] + place < cols)
    return jnp.where(inside, rms_silu(residual), 0.0).astype(BF16)


def column_taps(weights):
    return jnp.concatenate(
        [jnp.concatenate([weight[c] for c in range(weight.shape[0])], axis=1) for weight in weights],
        axis=0,
    )


def inner_kernel(
    cols,
    place_in_mesh,
    main,
    conv_win,
    early,
    weight,
    head,
    late,
    head_rows,
    normed,
    inner,
    head_in,
    sums,
    sems,
):
    frames, rows, win, width = main.shape
    depth = head.shape[3]
    groups = late.shape[0] // GROUP

    def arriving(i):
        return pltpu.make_async_copy(
            weight.at[pl.ds(EARLY + GROUP * i, GROUP)], late.at[pl.ds(GROUP * i, GROUP)], sems.at[i]
        )

    head_copy = pltpu.make_async_copy(head, head_in, sems.at[groups])
    for i in range(groups):
        arriving(i).start()
        if i == 0:
            head_copy.start()
    normed[0:2] = conv_win[...]
    normed[2:] = rms_silu(main[...].astype(F32)).astype(BF16)
    head_rows[...] = jnp.zeros_like(head_rows)
    count = frames * (rows - 2) * win

    def product(pairs, weights):
        left = jnp.concatenate(
            [
                normed[pl.ds(pair // 3, frames), pl.ds(pair % 3, rows - 2)].reshape(count, width)
                for pair in pairs
            ],
            axis=1,
        )
        return jnp.dot(left, column_taps(weights), preferred_element_type=F32)

    sums[...] = product(range(EARLY), [early[i] for i in range(EARLY)])

    def step(i, carry):
        arriving(i).wait()
        here = [GROUP * i + k for k in range(GROUP)]
        sums[...] += product([EARLY + k for k in here], [late[k] for k in here])

        @pl.when(i == 0)
        def _():
            head_copy.wait()
            for a in range(3):
                for b in range(3):
                    for c in range(3):
                        slot = 2 * a + c if c < 2 else 6 + a
                        start = slot * 64 + (2 - b) * depth
                        head_rows[start : start + depth] = head_in[a, b, c]

        return carry

    lax.fori_loop(0, groups, step, 0)
    own = main[:, 1 : rows - 1].astype(F32).reshape(count, width)
    inner[...] = after_block(sums[...], own, place_in_mesh, cols).reshape(inner.shape)


def section_kernel(
    cols, depth, place_in_mesh, main, near, far, head_win, early, late, head_rows, normed, inner, out, edges, hidden, pieces, sems
):
    frames, rows, win, width = main.shape
    count = frames * rows * win
    odd = place_in_mesh[1] % 2 == 1
    for edge, when_odd, when_even in ((0, near, far), (1, far, near)):
        edges[edge, 0:2] = jnp.where(odd, when_odd[0:2], when_even[0:2])
        values = jnp.where(odd, when_odd[2:].astype(F32), when_even[2:].astype(F32))
        edges[edge, 2:] = rms_silu(values).astype(BF16)
    hidden[0:2] = head_win[...]
    hidden[2:, 1 : rows - 1] = inner[...]

    def both(first, second):
        return jnp.concatenate([first[:, None], second[:, None]], axis=1).reshape(-1, width)

    columns = []
    for a in range(3):
        part = slice(a, a + frames)
        columns.append(both(edges[0, part], normed[part, rows - 2]))
        columns.append(both(normed[part, 0], normed[part, rows - 1]))
        columns.append(both(normed[part, 1], edges[1, part]))
    left = jnp.concatenate(columns, axis=1)
    weights = [early[i] for i in range(EARLY)] + [late[i] for i in range(late.shape[0])]
    sums = jnp.dot(left, column_taps(weights), preferred_element_type=F32)
    own = both(main[:, 0].astype(F32), main[:, rows - 1].astype(F32))
    outer = after_block(sums, own, place_in_mesh, cols).reshape(frames, 2, win, width)
    hidden[2:, 0] = outer[:, 0]
    hidden[2:, rows - 1] = outer[:, 1]

    before = rows * win
    taps = rows_times_rows(hidden[...].reshape(count + 2 * before, width), head_rows[...])
    pair = sum(taps[a * before : a * before + count, a * 128 : (a + 1) * 128] for a in range(3))
    last = taps[0:count, 384:512] + pltpu.roll(taps[before : before + count, 384:512], 64, 1)
    last += taps[2 * before : 2 * before + count, 512:576 + 64]
    total = pltpu.roll(pair, 2, 0) + pltpu.roll(pltpu.roll(pair, 64, 1), 1, 0) + last
    total = jnp.where(iota((1, 128), 1) < 64, total, 0.0).reshape(frames, rows, win, 128)
    copies = []
    for frame in range(frames):
        piece = total[frame, 0]
        for row in range(1, rows):
            piece += pltpu.roll(total[frame, row], depth * row, 1)
        piece = piece.astype(BF16)
        for target in range(out.shape[1]):
            pieces[frame, target] = piece
        copies.append(pltpu.make_async_copy(pieces.at[frame], out.at[frame], sems.at[frame]))
        copies[-1].start()
    for copy in copies:
        copy.wait()


def folded_kernel(patch, qkv, folded, gram, parts, qkv_in, sems):
    depth = patch.shape[2]
    width = patch.shape[3]
    positions = 4 * depth
    chunks = sems.shape[0]
    share = qkv.shape[0] // chunks
    def arriving(index):
        part = pl.ds(pl.multiple_of(index * share, 16), share)
        return part, pltpu.make_async_copy(qkv.at[part], qkv_in.at[part], sems.at[index])

    for index in range(chunks):
        arriving(index)[1].start()

    def stacked(values):
        pieces = list(three_parts(values))
        pieces.append(jnp.zeros_like(pieces[0]))
        return jnp.concatenate(pieces, axis=1)

    for b in range(2):
        for a in range(2):
            weights = patch[a, b].astype(F32)
            centred = weights - jnp.mean(weights, axis=1, keepdims=True)
            for index, part in enumerate(three_parts(centred)):
                start = index * positions + (2 * b + a) * depth
                parts[start : start + depth] = part
    product = rows_times_rows(parts[...], parts[...])
    total = jnp.zeros((positions, positions), F32)
    for i in range(3):
        for k in range(3):
            total += product[
                i * positions : (i + 1) * positions, k * positions : (k + 1) * positions
            ]
    gram[...] = stacked(total / width)

    def step(index, carry):
        part, copy = arriving(index)
        copy.wait()
        product = rows_times_rows(qkv_in[part], parts[...])
        folded[part] = stacked(
            product[:, :positions]
            + product[:, positions : 2 * positions]
            + product[:, 2 * positions :]
        )
        return carry

    lax.fori_loop(0, chunks, step, 0)


def project_kernel(depth, pieces, folded, gram, out, sums, patches, columns, staged, sems):
    groups, blocks, win, lanes = pieces.shape
    positions = 4 * depth
    tokens = patches.shape[0]
    half = tokens // (2 * blocks)
    pad = (half + 7) // 8 * 8

    shape = (2 * pad, groups * win)
    row = iota(shape, 0)
    place = iota(shape, 1)
    odd = (row >= pad).astype(jnp.int32)
    patch_col = row - pad * odd
    column = STEP * (place // win) + place % win - 1
    pick = ((column == 2 * patch_col + odd) & (patch_col < half)).astype(BF16)
    for block in range(blocks):
        source = pieces[:, block].reshape(groups * win, lanes)
        sums[block] = jnp.dot(pick, source, preferred_element_type=F32)
    slot = iota((1, lanes), 1) // depth
    turned = [None] * blocks
    for block in range(blocks):
        for near in (block, block + 1):
            if near < blocks and turned[near] is None:
                turned[near] = pltpu.roll(sums[near], 4 * depth, 1)
        total = sums[block]
        if block > 0:
            total += jnp.where(slot == 1, turned[block - 1], 0.0)
        if block < blocks - 1:
            total += jnp.where(slot == 4, turned[block + 1], 0.0)
        for i in range(2):
            start = (1 + 2 * i) * depth
            even = pltpu.roll(total[0:pad], lanes - start, 1)
            uneven = pltpu.roll(total[pad:], (lanes + 2 * depth - start) % lanes, 1)
            patch = jnp.where(slot < 2, even, jnp.where(slot < 4, uneven, 0.0))
            first = (2 * block + i) * half
            patches[first : first + half] = patch[0:half]
    turned = jnp.transpose(patches[...])[0:positions]
    rounded = turned.astype(BF16)
    for index in range(4):
        columns[index * positions : (index + 1) * positions] = rounded
    product = jnp.dot(gram[...], columns[...], preferred_element_type=F32)
    variance = jnp.sum(product * rounded.astype(F32), axis=0, keepdims=True)
    scale = lax.rsqrt(jnp.maximum(variance, 0.0) + EPS)
    chunks = sems.shape[0]
    share = folded.shape[0] // chunks
    copies = []
    for index in range(chunks):
        part = pl.ds(index * share, share)
        product = jnp.dot(folded[part], columns[...], preferred_element_type=F32)
        staged[part] = (product * scale).astype(BF16)
        copies.append(pltpu.make_async_copy(staged.at[part], out.at[part], sems.at[index]))
        copies[-1].start()
    for copy in copies:
        copy.wait()


ON_CHIP = pl.BlockSpec(memory_space=pltpu.VMEM)
IN_HBM = pl.BlockSpec(memory_space=pltpu.HBM)
SCALAR = pl.BlockSpec(memory_space=pltpu.SMEM)


def params(mebibytes):
    return pltpu.CompilerParams(vmem_limit_bytes=mebibytes << 20)


def in_hbm(array):
    return pltpu.with_memory_space_constraint(array, pltpu.HBM)


def feature_windows(features, groups):
    rows, cols, width = features.shape
    return pl.pallas_call(
        functools.partial(feature_windows_kernel, groups),
        in_specs=[IN_HBM],
        out_specs=IN_HBM,
        out_shape=pltpu.HBM((groups, rows, WIN, width), BF16),
        scratch_shapes=[
            pltpu.VMEM(features.shape, BF16),
            pltpu.VMEM((groups, rows, WIN, width), BF16),
            pltpu.SemaphoreType.DMA((rows,)),
            pltpu.SemaphoreType.DMA((rows,)),
        ],
        compiler_params=params(8),
        name="feature_windows",
    )(in_hbm(features))


def cache_windows(position, conv_cache, head_cache, weight):
    frames, rows, cols, width = conv_cache.shape
    window = pltpu.VMEM((frames, rows, WIN, width), BF16)
    return pl.pallas_call(
        cache_windows_kernel,
        in_specs=[SCALAR, IN_HBM, IN_HBM, IN_HBM],
        out_specs=[ON_CHIP] * 3,
        out_shape=[window, window, pltpu.VMEM((EARLY,) + weight.shape[1:], BF16)],
        scratch_shapes=[
            pltpu.VMEM(conv_cache.shape, BF16),
            pltpu.VMEM(head_cache.shape, BF16),
            pltpu.SemaphoreType.DMA((3,)),
        ],
        compiler_params=params(8),
        name="cache_windows",
    )(position, in_hbm(conv_cache), in_hbm(head_cache), in_hbm(weight))


def inner_rows(place_in_mesh, main, conv_win, early, weight, head, cols):
    frames, rows, win, width = main.shape
    late = (weight.shape[0] - EARLY,) + weight.shape[1:]
    return pl.pallas_call(
        functools.partial(inner_kernel, cols),
        in_specs=[SCALAR] + [ON_CHIP] * 3 + [IN_HBM] * 2,
        out_specs=[ON_CHIP] * 4,
        out_shape=[
            pltpu.VMEM(late, BF16),
            pltpu.VMEM((10 * 64, width), BF16),
            pltpu.VMEM((frames + 2, rows, win, width), BF16),
            pltpu.VMEM((frames, rows - 2, win, width), BF16),
        ],
        scratch_shapes=[
            pltpu.VMEM(head.shape, BF16),
            pltpu.VMEM((frames * (rows - 2) * win, 3 * width), F32),
            pltpu.SemaphoreType.DMA((late[0] // GROUP + 1,)),
        ],
        compiler_params=params(20),
        name="inner_rows",
    )(place_in_mesh, main, conv_win, early, in_hbm(weight), in_hbm(head))


def section(place_in_mesh, main, near, far, head_win, early, prepared, cols, depth, blocks):
    frames, rows, win, width = main.shape
    return pl.pallas_call(
        functools.partial(section_kernel, cols, depth),
        in_specs=[SCALAR] + [ON_CHIP] * 9,
        out_specs=IN_HBM,
        out_shape=pltpu.HBM((frames, blocks, win, 128), BF16),
        scratch_shapes=[
            pltpu.VMEM((2, frames + 2, win, width), BF16),
            pltpu.VMEM((frames + 2, rows, win, width), BF16),
            pltpu.VMEM((frames, blocks, win, 128), BF16),
            pltpu.SemaphoreType.DMA((frames,)),
        ],
        compiler_params=params(20),
        name="section",
    )(place_in_mesh, main, near, far, head_win, early, *prepared)


def folded_weights(patch, qkv):
    positions = 4 * patch.shape[2]
    chunks = 4
    return pl.pallas_call(
        folded_kernel,
        in_specs=[ON_CHIP, IN_HBM],
        out_specs=[ON_CHIP] * 2,
        out_shape=[
            pltpu.VMEM((qkv.shape[0], 4 * positions), BF16),
            pltpu.VMEM((positions, 4 * positions), BF16),
        ],
        scratch_shapes=[
            pltpu.VMEM((3 * positions, patch.shape[3]), BF16),
            pltpu.VMEM(qkv.shape, BF16),
            pltpu.SemaphoreType.DMA((chunks,)),
        ],
        compiler_params=params(24),
        name="folded_weights",
    )(patch, in_hbm(qkv))


def project(pieces, folded, gram, cols, depth):
    groups, blocks, win, lanes = pieces.shape
    half = cols // 2
    pad = (half + 7) // 8 * 8
    tokens = 2 * blocks * half
    outputs = folded.shape[0]
    chunks = 4
    return pl.pallas_call(
        functools.partial(project_kernel, depth),
        in_specs=[ON_CHIP] * 3,
        out_specs=IN_HBM,
        out_shape=pltpu.HBM((outputs, tokens), BF16),
        scratch_shapes=[
            pltpu.VMEM((blocks, 2 * pad, lanes), F32),
            pltpu.VMEM((tokens, lanes), F32),
            pltpu.VMEM((16 * depth, tokens), BF16),
            pltpu.VMEM((outputs, tokens), BF16),
            pltpu.SemaphoreType.DMA((chunks,)),
        ],
        compiler_params=params(20),
        name="project",
    )(pieces, folded, gram)


def swaps(count, first):
    pairs = [(i, i + 1) for i in range(first, count - 1, 2)]
    return pairs + [(target, source) for source, target in pairs]


def local(features, conv_cache, head_cache, conv_weight, head_weight, patch_weight, qkv_weight):
    groups = lax.axis_size("tm")
    blocks = lax.axis_size("rows")
    _, rows, cols, width = features.shape
    depth = head_weight.shape[-1]
    local_cols = qkv_weight.shape[2]
    block = lax.axis_index("rows")
    place_in_mesh = jnp.stack([lax.axis_index("tm"), block]).astype(jnp.int32)
    head = head_weight.transpose(0, 1, 2, 4, 3)
    flat_qkv = qkv_weight.transpose(1, 2, 0).reshape(3 * local_cols, qkv_weight.shape[0])

    main = lax.all_to_all(feature_windows(features[0], groups), "tm", 0, 0, tiled=True)
    pairs = conv_weight.reshape((9,) + conv_weight.shape[2:])
    conv_win, head_win, early = cache_windows(place_in_mesh, conv_cache, head_cache, pairs)
    def edge(row):
        return jnp.concatenate(
            [lax.dynamic_index_in_dim(part, row, 1, False) for part in (conv_win, main)]
        )

    odd = block % 2
    far = lax.ppermute(edge((rows - 1) * odd), "rows", swaps(blocks, 1))
    near = lax.ppermute(edge((rows - 1) * (1 - odd)), "rows", swaps(blocks, 0))
    prepared = inner_rows(place_in_mesh, main, conv_win, early, pairs, head, cols)
    partial = section(
        place_in_mesh, main, near, far, head_win, early, prepared, cols, depth, blocks
    )
    pieces = lax.all_to_all(
        partial.reshape(groups * blocks, WIN, 128), ("tm", "rows"), 0, 0, tiled=True
    ).reshape(groups, blocks, WIN, 128)
    folded, gram = folded_weights(patch_weight, flat_qkv)
    result = project(pieces, folded, gram, cols, depth)
    return result.reshape(3, local_cols, result.shape[1]).transpose(2, 0, 1)


def solution(mesh):
    return jax.shard_map(
        local,
        mesh=mesh,
        in_specs=(
            P("tm", "rows", None, None),
            P(None, "rows", None, None),
            P(None, "rows", None, None),
            P(),
            P(),
            P(),
            P(None, None, "rows"),
        ),
        out_specs=P("tm", None, "rows"),
        check_vma=False,
    )
```

```python
import functools

import jax
import jax.numpy as jnp
from jax import lax
from jax.experimental import pallas as pl
from jax.experimental.pallas import tpu as pltpu
from jax.sharding import PartitionSpec as P

F32 = jnp.float32
BF16 = jnp.bfloat16
EPS = 1e-06
STEP = 14
EARLY = 3
GROUP = 2
WIN = 16


def iota(shape, axis):
    return lax.broadcasted_iota(jnp.int32, shape, axis)


def rms_silu(values):
    scaled = values * lax.rsqrt(jnp.mean(values * values, axis=-1, keepdims=True) + EPS)
    return scaled / (1.0 + jnp.exp(-scaled))


def three_parts(values):
    first = values.astype(BF16)
    rest = values - first.astype(F32)
    second = rest.astype(BF16)
    third = (rest - second.astype(F32)).astype(BF16)
    return first, second, third


def rows_times_rows(left, right):
    return lax.dot_general(left, right, (((1,), (1,)), ((), ())), preferred_element_type=F32)


def feature_windows_kernel(groups, features, send, rows_in, windows, sems_in, sems_out):
    rows, cols, width = features.shape
    copies = [
        pltpu.make_async_copy(features.at[row], rows_in.at[row], sems_in.at[row])
        for row in range(rows)
    ]
    for copy in copies:
        copy.start()
    after = STEP * (groups - 1) + WIN - 1 - cols
    results = []
    for row in range(rows):
        copies[row].wait()
        values = jnp.concatenate(
            [
                jnp.zeros((8, width), F32),
                rows_in[row].astype(F32),
                jnp.zeros(((after + 7) // 8 * 8, width), F32),
            ],
            axis=0,
        )
        for group in range(groups):
            first = 8 + STEP * group - 1
            windows[group, row] = values[first : first + WIN].astype(BF16)
        part = pl.ds(row, 1)
        results.append(
            pltpu.make_async_copy(windows.at[:, part], send.at[:, part], sems_out.at[row])
        )
        results[-1].start()
    for copy in results:
        copy.wait()


def cache_windows_kernel(
    position, conv_cache, head_cache, weight, conv_win, head_win, early, conv_in, head_in, sems
):
    frames, rows, cols, _ = conv_cache.shape
    copies = [
        pltpu.make_async_copy(conv_cache, conv_in, sems.at[0]),
        pltpu.make_async_copy(head_cache, head_in, sems.at[1]),
        pltpu.make_async_copy(weight.at[pl.ds(0, early.shape[0])], early, sems.at[2]),
    ]
    for copy in copies:
        copy.start()
    shape = (WIN, cols)
    place = iota(shape, 0)
    first = STEP * position[0]
    pick_conv = (iota(shape, 1) == first + place - 1).astype(BF16)
    pick_head = ((iota(shape, 1) == first + place) & (place < STEP)).astype(BF16)
    for copy, pick, source, out in (
        (copies[0], pick_conv, conv_in, conv_win),
        (copies[1], pick_head, head_in, head_win),
    ):
        copy.wait()
        for frame in range(frames):
            for row in range(rows):
                out[frame, row] = jnp.dot(
                    pick, source[frame, row], preferred_element_type=F32
                ).astype(BF16)
    copies[2].wait()


def after_block(sums, features, place_in_mesh, cols):
    count, width = features.shape
    update = (
        sums[:, :width]
        + pltpu.roll(sums[:, width : 2 * width], count - 1, 0)
        + pltpu.roll(sums[:, 2 * width :], count - 2, 0)
    )
    residual = (pltpu.roll(features, count - 1, 0) + update).astype(BF16).astype(F32)
    place = iota((count, 1), 0) % WIN
    inside = (place < STEP) & (STEP * place_in_mesh[0] + place < cols)
    return jnp.where(inside, rms_silu(residual), 0.0).astype(BF16)


def column_taps(weights):
    return jnp.concatenate(
        [jnp.concatenate([weight[c] for c in range(weight.shape[0])], axis=1) for weight in weights],
        axis=0,
    )


def inner_kernel(
    cols,
    place_in_mesh,
    main,
    conv_win,
    early,
    weight,
    head,
    late,
    head_rows,
    normed,
    inner,
    head_in,
    sums,
    sems,
):
    frames, rows, win, width = main.shape
    depth = head.shape[3]
    groups = late.shape[0] // GROUP

    def arriving(i):
        return pltpu.make_async_copy(
            weight.at[pl.ds(EARLY + GROUP * i, GROUP)], late.at[pl.ds(GROUP * i, GROUP)], sems.at[i]
        )

    head_copy = pltpu.make_async_copy(head, head_in, sems.at[groups])
    for i in range(groups):
        arriving(i).start()
        if i == 0:
            head_copy.start()
    normed[0:2] = conv_win[...]
    normed[2:] = rms_silu(main[...].astype(F32)).astype(BF16)
    head_rows[...] = jnp.zeros_like(head_rows)
    count = frames * (rows - 2) * win

    def product(pairs, weights):
        left = jnp.concatenate(
            [
                normed[pl.ds(pair // 3, frames), pl.ds(pair % 3, rows - 2)].reshape(count, width)
                for pair in pairs
            ],
            axis=1,
        )
        return jnp.dot(left, column_taps(weights), preferred_element_type=F32)

    sums[...] = product(range(EARLY), [early[i] for i in range(EARLY)])

    def step(i, carry):
        arriving(i).wait()
        here = [GROUP * i + k for k in range(GROUP)]
        sums[...] += product([EARLY + k for k in here], [late[k] for k in here])

        @pl.when(i == 0)
        def _():
            head_copy.wait()
            for a in range(3):
                for b in range(3):
                    for c in range(3):
                        slot = 2 * a + c if c < 2 else 6 + a
                        start = slot * 64 + (2 - b) * depth
                        head_rows[start : start + depth] = head_in[a, b, c]

        return carry

    lax.fori_loop(0, groups, step, 0)
    own = main[:, 1 : rows - 1].astype(F32).reshape(count, width)
    inner[...] = after_block(sums[...], own, place_in_mesh, cols).reshape(inner.shape)


def section_kernel(
    cols, depth, place_in_mesh, main, near, far, head_win, early, late, head_rows, normed, inner, out, edges, pieces, sems
):
    frames, rows, win, width = main.shape
    count = frames * rows * win
    odd = place_in_mesh[1] % 2 == 1
    for edge, when_odd, when_even in ((0, near, far), (1, far, near)):
        edges[edge, 0:2] = jnp.where(odd, when_odd[0:2], when_even[0:2])
        values = jnp.where(odd, when_odd[2:].astype(F32), when_even[2:].astype(F32))
        edges[edge, 2:] = rms_silu(values).astype(BF16)
    lanes = head_rows.shape[0]

    def head_taps(values):
        product = rows_times_rows(values.reshape(-1, width), head_rows[...])
        return product.reshape(values.shape[:3] + (lanes,))

    cached_taps = head_taps(head_win[...])
    inner_taps = head_taps(inner[...])

    def both(first, second):
        return jnp.concatenate([first[:, None], second[:, None]], axis=1).reshape(-1, width)

    columns = []
    for a in range(3):
        part = slice(a, a + frames)
        columns.append(both(edges[0, part], normed[part, rows - 2]))
        columns.append(both(normed[part, 0], normed[part, rows - 1]))
        columns.append(both(normed[part, 1], edges[1, part]))
    left = jnp.concatenate(columns, axis=1)
    weights = [early[i] for i in range(EARLY)] + [late[i] for i in range(late.shape[0])]
    sums = jnp.dot(left, column_taps(weights), preferred_element_type=F32)
    own = both(main[:, 0].astype(F32), main[:, rows - 1].astype(F32))
    outer = after_block(sums, own, place_in_mesh, cols).reshape(frames, 2, win, width)
    outer_taps = head_taps(outer)

    before = rows * win
    taps = jnp.concatenate([outer_taps[:, 0:1], inner_taps, outer_taps[:, 1:2]], axis=1)
    taps = jnp.concatenate([cached_taps, taps], axis=0).reshape(count + 2 * before, lanes)
    pair = sum(taps[a * before : a * before + count, a * 128 : (a + 1) * 128] for a in range(3))
    last = taps[0:count, 384:512] + pltpu.roll(taps[before : before + count, 384:512], 64, 1)
    last += taps[2 * before : 2 * before + count, 512:576 + 64]
    total = pltpu.roll(pair, 2, 0) + pltpu.roll(pltpu.roll(pair, 64, 1), 1, 0) + last
    total = jnp.where(iota((1, 128), 1) < 64, total, 0.0).reshape(frames, rows, win, 128)
    copies = []
    for frame in range(frames):
        piece = total[frame, 0]
        for row in range(1, rows):
            piece += pltpu.roll(total[frame, row], depth * row, 1)
        piece = piece.astype(BF16)
        for target in range(out.shape[1]):
            pieces[frame, target] = piece
        copies.append(pltpu.make_async_copy(pieces.at[frame], out.at[frame], sems.at[frame]))
        copies[-1].start()
    for copy in copies:
        copy.wait()


def folded_kernel(patch, qkv, folded, gram, parts, qkv_in, sems):
    depth = patch.shape[2]
    width = patch.shape[3]
    positions = 4 * depth
    chunks = sems.shape[0]
    share = qkv.shape[0] // chunks
    def arriving(index):
        part = pl.ds(pl.multiple_of(index * share, 16), share)
        return part, pltpu.make_async_copy(qkv.at[part], qkv_in.at[part], sems.at[index])

    for index in range(chunks):
        arriving(index)[1].start()

    def stacked(values):
        pieces = list(three_parts(values))
        pieces.append(jnp.zeros_like(pieces[0]))
        return jnp.concatenate(pieces, axis=1)

    for b in range(2):
        for a in range(2):
            weights = patch[a, b].astype(F32)
            centred = weights - jnp.mean(weights, axis=1, keepdims=True)
            for index, part in enumerate(three_parts(centred)):
                start = index * positions + (2 * b + a) * depth
                parts[start : start + depth] = part
    product = rows_times_rows(parts[...], parts[...])
    total = jnp.zeros((positions, positions), F32)
    for i in range(3):
        for k in range(3):
            total += product[
                i * positions : (i + 1) * positions, k * positions : (k + 1) * positions
            ]
    gram[...] = stacked(total / width)

    def step(index, carry):
        part, copy = arriving(index)
        copy.wait()
        product = rows_times_rows(qkv_in[part], parts[...])
        folded[part] = stacked(
            product[:, :positions]
            + product[:, positions : 2 * positions]
            + product[:, 2 * positions :]
        )
        return carry

    lax.fori_loop(0, chunks, step, 0)


def project_kernel(depth, pieces, folded, gram, out, sums, patches, columns, staged, sems):
    groups, blocks, win, lanes = pieces.shape
    positions = 4 * depth
    tokens = patches.shape[0]
    half = tokens // (2 * blocks)
    pad = (half + 7) // 8 * 8

    shape = (2 * pad, groups * win)
    row = iota(shape, 0)
    place = iota(shape, 1)
    odd = (row >= pad).astype(jnp.int32)
    patch_col = row - pad * odd
    column = STEP * (place // win) + place % win - 1
    pick = ((column == 2 * patch_col + odd) & (patch_col < half)).astype(BF16)
    for block in range(blocks):
        source = pieces[:, block].reshape(groups * win, lanes)
        sums[block] = jnp.dot(pick, source, preferred_element_type=F32)
    slot = iota((1, lanes), 1) // depth
    turned = [None] * blocks
    for block in range(blocks):
        for near in (block, block + 1):
            if near < blocks and turned[near] is None:
                turned[near] = pltpu.roll(sums[near], 4 * depth, 1)
        total = sums[block]
        if block > 0:
            total += jnp.where(slot == 1, turned[block - 1], 0.0)
        if block < blocks - 1:
            total += jnp.where(slot == 4, turned[block + 1], 0.0)
        for i in range(2):
            start = (1 + 2 * i) * depth
            even = pltpu.roll(total[0:pad], lanes - start, 1)
            uneven = pltpu.roll(total[pad:], (lanes + 2 * depth - start) % lanes, 1)
            patch = jnp.where(slot < 2, even, jnp.where(slot < 4, uneven, 0.0))
            first = (2 * block + i) * half
            patches[first : first + half] = patch[0:half]
    turned = jnp.transpose(patches[...])[0:positions]
    rounded = turned.astype(BF16)
    for index in range(4):
        columns[index * positions : (index + 1) * positions] = rounded
    product = jnp.dot(gram[...], columns[...], preferred_element_type=F32)
    variance = jnp.sum(product * rounded.astype(F32), axis=0, keepdims=True)
    scale = lax.rsqrt(jnp.maximum(variance, 0.0) + EPS)
    chunks = sems.shape[0]
    share = folded.shape[0] // chunks
    copies = []
    for index in range(chunks):
        part = pl.ds(index * share, share)
        product = jnp.dot(folded[part], columns[...], preferred_element_type=F32)
        staged[part] = (product * scale).astype(BF16)
        copies.append(pltpu.make_async_copy(staged.at[part], out.at[part], sems.at[index]))
        copies[-1].start()
    for copy in copies:
        copy.wait()


ON_CHIP = pl.BlockSpec(memory_space=pltpu.VMEM)
IN_HBM = pl.BlockSpec(memory_space=pltpu.HBM)
SCALAR = pl.BlockSpec(memory_space=pltpu.SMEM)


def params(mebibytes):
    return pltpu.CompilerParams(vmem_limit_bytes=mebibytes << 20)


def in_hbm(array):
    return pltpu.with_memory_space_constraint(array, pltpu.HBM)


def feature_windows(features, groups):
    rows, cols, width = features.shape
    return pl.pallas_call(
        functools.partial(feature_windows_kernel, groups),
        in_specs=[IN_HBM],
        out_specs=IN_HBM,
        out_shape=pltpu.HBM((groups, rows, WIN, width), BF16),
        scratch_shapes=[
            pltpu.VMEM(features.shape, BF16),
            pltpu.VMEM((groups, rows, WIN, width), BF16),
            pltpu.SemaphoreType.DMA((rows,)),
            pltpu.SemaphoreType.DMA((rows,)),
        ],
        compiler_params=params(8),
        name="feature_windows",
    )(in_hbm(features))


def cache_windows(position, conv_cache, head_cache, weight):
    frames, rows, cols, width = conv_cache.shape
    window = pltpu.VMEM((frames, rows, WIN, width), BF16)
    return pl.pallas_call(
        cache_windows_kernel,
        in_specs=[SCALAR, IN_HBM, IN_HBM, IN_HBM],
        out_specs=[ON_CHIP] * 3,
        out_shape=[window, window, pltpu.VMEM((EARLY,) + weight.shape[1:], BF16)],
        scratch_shapes=[
            pltpu.VMEM(conv_cache.shape, BF16),
            pltpu.VMEM(head_cache.shape, BF16),
            pltpu.SemaphoreType.DMA((3,)),
        ],
        compiler_params=params(8),
        name="cache_windows",
    )(position, in_hbm(conv_cache), in_hbm(head_cache), in_hbm(weight))


def inner_rows(place_in_mesh, main, conv_win, early, weight, head, cols):
    frames, rows, win, width = main.shape
    late = (weight.shape[0] - EARLY,) + weight.shape[1:]
    return pl.pallas_call(
        functools.partial(inner_kernel, cols),
        in_specs=[SCALAR] + [ON_CHIP] * 3 + [IN_HBM] * 2,
        out_specs=[ON_CHIP] * 4,
        out_shape=[
            pltpu.VMEM(late, BF16),
            pltpu.VMEM((10 * 64, width), BF16),
            pltpu.VMEM((frames + 2, rows, win, width), BF16),
            pltpu.VMEM((frames, rows - 2, win, width), BF16),
        ],
        scratch_shapes=[
            pltpu.VMEM(head.shape, BF16),
            pltpu.VMEM((frames * (rows - 2) * win, 3 * width), F32),
            pltpu.SemaphoreType.DMA((late[0] // GROUP + 1,)),
        ],
        compiler_params=params(20),
        name="inner_rows",
    )(place_in_mesh, main, conv_win, early, in_hbm(weight), in_hbm(head))


def section(place_in_mesh, main, near, far, head_win, early, prepared, cols, depth, blocks):
    frames, rows, win, width = main.shape
    return pl.pallas_call(
        functools.partial(section_kernel, cols, depth),
        in_specs=[SCALAR] + [ON_CHIP] * 9,
        out_specs=IN_HBM,
        out_shape=pltpu.HBM((frames, blocks, win, 128), BF16),
        scratch_shapes=[
            pltpu.VMEM((2, frames + 2, win, width), BF16),
            pltpu.VMEM((frames, blocks, win, 128), BF16),
            pltpu.SemaphoreType.DMA((frames,)),
        ],
        compiler_params=params(20),
        name="section",
    )(place_in_mesh, main, near, far, head_win, early, *prepared)


def folded_weights(patch, qkv):
    positions = 4 * patch.shape[2]
    chunks = 4
    return pl.pallas_call(
        folded_kernel,
        in_specs=[ON_CHIP, IN_HBM],
        out_specs=[ON_CHIP] * 2,
        out_shape=[
            pltpu.VMEM((qkv.shape[0], 4 * positions), BF16),
            pltpu.VMEM((positions, 4 * positions), BF16),
        ],
        scratch_shapes=[
            pltpu.VMEM((3 * positions, patch.shape[3]), BF16),
            pltpu.VMEM(qkv.shape, BF16),
            pltpu.SemaphoreType.DMA((chunks,)),
        ],
        compiler_params=params(24),
        name="folded_weights",
    )(patch, in_hbm(qkv))


def project(pieces, folded, gram, cols, depth):
    groups, blocks, win, lanes = pieces.shape
    half = cols // 2
    pad = (half + 7) // 8 * 8
    tokens = 2 * blocks * half
    outputs = folded.shape[0]
    chunks = 4
    return pl.pallas_call(
        functools.partial(project_kernel, depth),
        in_specs=[ON_CHIP] * 3,
        out_specs=IN_HBM,
        out_shape=pltpu.HBM((outputs, tokens), BF16),
        scratch_shapes=[
            pltpu.VMEM((blocks, 2 * pad, lanes), F32),
            pltpu.VMEM((tokens, lanes), F32),
            pltpu.VMEM((16 * depth, tokens), BF16),
            pltpu.VMEM((outputs, tokens), BF16),
            pltpu.SemaphoreType.DMA((chunks,)),
        ],
        compiler_params=params(20),
        name="project",
    )(pieces, folded, gram)


def swaps(count, first):
    pairs = [(i, i + 1) for i in range(first, count - 1, 2)]
    return pairs + [(target, source) for source, target in pairs]


def local(features, conv_cache, head_cache, conv_weight, head_weight, patch_weight, qkv_weight):
    groups = lax.axis_size("tm")
    blocks = lax.axis_size("rows")
    _, rows, cols, width = features.shape
    depth = head_weight.shape[-1]
    local_cols = qkv_weight.shape[2]
    block = lax.axis_index("rows")
    place_in_mesh = jnp.stack([lax.axis_index("tm"), block]).astype(jnp.int32)
    head = head_weight.transpose(0, 1, 2, 4, 3)
    flat_qkv = qkv_weight.transpose(1, 2, 0).reshape(3 * local_cols, qkv_weight.shape[0])

    main = lax.all_to_all(feature_windows(features[0], groups), "tm", 0, 0, tiled=True)
    pairs = conv_weight.reshape((9,) + conv_weight.shape[2:])
    conv_win, head_win, early = cache_windows(place_in_mesh, conv_cache, head_cache, pairs)
    def edge(row):
        return jnp.concatenate(
            [lax.dynamic_index_in_dim(part, row, 1, False) for part in (conv_win, main)]
        )

    odd = block % 2
    far = lax.ppermute(edge((rows - 1) * odd), "rows", swaps(blocks, 1))
    near = lax.ppermute(edge((rows - 1) * (1 - odd)), "rows", swaps(blocks, 0))
    prepared = inner_rows(place_in_mesh, main, conv_win, early, pairs, head, cols)
    partial = section(
        place_in_mesh, main, near, far, head_win, early, prepared, cols, depth, blocks
    )
    pieces = lax.all_to_all(
        partial.reshape(groups * blocks, WIN, 128), ("tm", "rows"), 0, 0, tiled=True
    ).reshape(groups, blocks, WIN, 128)
    folded, gram = folded_weights(patch_weight, flat_qkv)
    result = project(pieces, folded, gram, cols, depth)
    return result.reshape(3, local_cols, result.shape[1]).transpose(2, 0, 1)


def solution(mesh):
    return jax.shard_map(
        local,
        mesh=mesh,
        in_specs=(
            P("tm", "rows", None, None),
            P(None, "rows", None, None),
            P(None, "rows", None, None),
            P(),
            P(),
            P(),
            P(None, None, "rows"),
        ),
        out_specs=P("tm", None, "rows"),
        check_vma=False,
    )
```
